32 devices in a mesh: expert: 8 (over z, y), tensor: 4 (over x, core).
Axes of the slice: x: 2, y: 2, z: 4, core: 2. Of those that a mesh axis runs over, the one named last changes fastest.
Arguments:
- grad_out: bfloat16 [1024, 4096], P('expert', 'tensor'), may hold values from -0.796875 to 0.796875
- gate_weights: bfloat16 [1024, 8], P('expert'), may hold values from 0.049804688 to 1
- slot_lists: int32 [8, 8, 128], P('expert'), may hold values from -1 to 1023, as said below
- saved_gate: bfloat16 [8, 1024, 1536], P('expert', None, 'tensor'), may hold values from -6 to 6
- saved_up: bfloat16 [8, 1024, 1536], P('expert', None, 'tensor'), may hold values from -6 to 6
- w_gate: bfloat16 [8, 4096, 1536], P('expert', None, 'tensor'), may hold values from -0.09375 to 0.09375
- w_up: bfloat16 [8, 4096, 1536], P('expert', None, 'tensor'), may hold values from -0.09375 to 0.09375
- w_down: bfloat16 [8, 1536, 4096], P('expert', 'tensor'), may hold values from -0.15625 to 0.15625
Outputs:
- grad_in: bfloat16 [1024, 4096], P('expert', 'tensor')
- grad_gate: float32 [1024, 8], P('expert')
The draws below stay inside these ranges and needn't reach their ends.
Inputs may be any that keep to these rules, and one draw needn't show every extreme that they name: slot_lists[s, e, c] is t * 8 + k where expert e is the k-th of the 8 different experts chosen by token t of group s, or -1 for an empty slot; every pair (t, k) of a group stands in exactly one slot, the live slots of each list come first, and in every draw one expert's list holds 128 live entries from every group.
All inputs are finite; a program needn't handle non-finite values.
Results may differ from the reference program's by a relative error of at most 0.012.
Values may be sent and summed in bfloat16 or wider, within the bound.
No kernel may reach another device: no remote copies, remote signals or barrier semaphores. Data moves between devices by JAX's collectives and lax.ppermute only.
A program may use at most 128 MiB of HBM per device.

```python
import math
import jax
import jax.numpy as jnp
from jax import lax

D = 4096
FF = 1536
TOPK = 8
TOK_DEV = 128
EXPERTS = 8
TOKENS = 1024
CAP = 128
SLOTS = 1024
FL = 384
N_TENSOR = 4


def routing_table(key):
    group_count = TOKENS // TOK_DEV
    shared_hot = jax.random.randint(jax.random.fold_in(key, 11), (), 0, EXPERTS).astype(jnp.int32)
    expert_ids = jnp.arange(EXPERTS, dtype=jnp.int32)

    def one_group(group_key):
        key_pop, key_hot, key_noise, key_ties = jax.random.split(group_key, 4)
        popular = jax.random.randint(key_pop, (EXPERTS,), 0, 6).astype(jnp.int32)
        local_hot = jax.random.randint(key_hot, (), 0, EXPERTS).astype(jnp.int32)
        popular = popular + jnp.where(expert_ids == shared_hot, 4096, 0) + jnp.where(expert_ids == local_hot, 2048, 0)
        noise = jax.random.randint(key_noise, (TOK_DEV, EXPERTS), 0, 8).astype(jnp.int32)
        ties = jax.random.permutation(key_ties, EXPERTS).astype(jnp.int32)

        def pick_step(counts, noise_row):
            score = (popular + noise_row) * EXPERTS + ties
            score = jnp.where(counts < CAP, score, -1 - ties)
            unused, chosen = lax.top_k(score, TOPK)
            chosen = chosen.astype(jnp.int32)
            placed = counts[chosen]
            counts = counts.at[chosen].add(1)
            return (counts, (chosen, placed))
        unused, (chosen, placed) = lax.scan(pick_step, jnp.zeros((EXPERTS,), jnp.int32), noise)
        entries = (jnp.arange(TOK_DEV, dtype=jnp.int32)[:, None] * TOPK + jnp.arange(TOPK, dtype=jnp.int32)[None, :]).astype(jnp.int32)
        empty_table = jnp.full((EXPERTS, CAP), -1, jnp.int32)
        return empty_table.at[chosen.reshape(-1), placed.reshape(-1)].set(entries.reshape(-1))
    group_keys = jax.random.split(jax.random.fold_in(key, 7), group_count)
    return jax.vmap(one_group)(group_keys)


def draw_slot_lists(key, part):
    return routing_table(key)


def block_scale(rng, dims, cuts, low, largest):
    def one(position, shards_of):
        draws = jax.random.uniform(jax.random.fold_in(jax.random.fold_in(rng, 6), position), (shards_of,), jnp.float32, low / len(cuts), largest / len(cuts))
        return jnp.repeat(jnp.exp(draws), dims[position] // shards_of).reshape((-1,) + (1,) * (len(dims) - position - 1))

    loudness = one(*cuts[0])
    for cut in cuts[1:]:
        loudness = loudness * one(*cut)
    return loudness


def gaussian(rng, extent, spread, most, pieces=(), held_as=jnp.bfloat16):
    values = spread * jax.random.normal(rng, extent, jnp.float32)
    if pieces:
        values = values * block_scale(rng, extent, pieces, -0.22, 0.18)
    return jnp.clip(values, -most, most).astype(held_as)


def setup_inputs(seed: int = 0) -> dict:
    keys = jax.random.split(jax.random.key(seed), 9)
    return {
        "grad_out": gaussian(keys[0], (TOKENS, D), 0.1, 0.796875, ((0, 8), (1, 4))),
        "gate_weights": jnp.clip(jnp.exp(math.log(1.0) - 2.9996462 * jax.random.uniform(keys[1], (TOKENS, TOPK), jnp.float32) ** block_scale(keys[1], (TOKENS, TOPK), ((0, 8),), -0.2, 0.2)), 0.049804688, 1.0).astype(jnp.bfloat16),
        "slot_lists": draw_slot_lists(jax.random.fold_in(keys[8], 71), 0),
        "saved_gate": gaussian(keys[3], (EXPERTS, SLOTS, FF), 1.0, 6.0, ((0, 8), (2, 4))),
        "saved_up": gaussian(keys[4], (EXPERTS, SLOTS, FF), 1.0, 6.0, ((0, 8), (2, 4))),
        "w_gate": gaussian(keys[5], (EXPERTS, D, FF), D ** -0.5, 0.09375, ((0, 8), (2, 4))),
        "w_up": gaussian(keys[6], (EXPERTS, D, FF), D ** -0.5, 0.09375, ((0, 8), (2, 4))),
        "w_down": gaussian(keys[7], (EXPERTS, FF, D), FF ** -0.5, 0.15625, ((0, 8), (1, 4))),
    }


def silu_pair(pre_act):
    sigma = jax.nn.sigmoid(pre_act)
    return pre_act * sigma, sigma * (1.0 + pre_act * (1.0 - sigma))


def reference(grad_out, gate_weights, slot_lists, saved_gate, saved_up, w_gate, w_up, w_down):
    groups = slot_lists.shape[0]
    slot_order = jnp.transpose(slot_lists, (1, 0, 2)).reshape(EXPERTS, groups * CAP)
    source_base = jnp.broadcast_to((jnp.arange(groups, dtype=jnp.int32) * TOK_DEV)[:, None], (groups, CAP)).reshape(-1)
    occupied = slot_order >= 0
    safe_entry = jnp.where(occupied, slot_order, 0).astype(jnp.int32)
    token_rows = (source_base[None, :] + safe_entry // TOPK).astype(jnp.int32)
    flat_slots = (source_base[None, :] * TOPK + safe_entry).astype(jnp.int32)
    gate_flat = gate_weights.reshape(-1)

    def expert_step(carry, inputs):
        grad_acc, gate_acc = carry
        tok_index, flat_index, alive, pre_gate, pre_up, gate_proj, up_proj, down_proj = inputs
        routed = jnp.where(alive[:, None], grad_out[tok_index], jnp.zeros((), grad_out.dtype)).astype(jnp.bfloat16)
        slot_gates = jnp.where(alive, gate_flat[flat_index].astype(jnp.float32), jnp.zeros((), jnp.float32))
        back_hidden = jnp.dot(routed, down_proj.T, preferred_element_type=jnp.float32)
        gate_pre = pre_gate.astype(jnp.float32)
        up_pre = pre_up.astype(jnp.float32)
        activated, derivative = silu_pair(gate_pre)
        hidden = activated * up_pre
        slot_gate_grad = jnp.sum(back_hidden * hidden, axis=1)
        scaled = slot_gates[:, None] * back_hidden
        grad_pre_gate = (scaled * up_pre * derivative).astype(jnp.bfloat16)
        grad_pre_up = (scaled * activated).astype(jnp.bfloat16)
        running = jnp.zeros((routed.shape[0], D), jnp.float32)
        for block in range(N_TENSOR):
            lower_end = block * FL
            upper_end = lower_end + FL
            block_sum = jnp.dot(grad_pre_gate[:, lower_end:upper_end], gate_proj[:, lower_end:upper_end].T, preferred_element_type=jnp.float32)
            block_sum = block_sum + jnp.dot(grad_pre_up[:, lower_end:upper_end], up_proj[:, lower_end:upper_end].T, preferred_element_type=jnp.float32)
            running = running + lax.optimization_barrier(block_sum.astype(jnp.bfloat16)).astype(jnp.float32)
        grad_acc = grad_acc.at[tok_index].add(jnp.where(alive[:, None], running, jnp.zeros((), jnp.float32)))
        gate_acc = gate_acc.at[flat_index].add(jnp.where(alive, slot_gate_grad, jnp.zeros((), jnp.float32)))
        return (grad_acc, gate_acc), None

    initial = (jnp.zeros((TOKENS, D), jnp.float32), jnp.zeros((TOKENS * TOPK,), jnp.float32))
    (grad_acc, gate_acc), _ = lax.scan(expert_step, initial, (token_rows, flat_slots, occupied, saved_gate, saved_up, w_gate, w_up, w_down))
    return grad_acc.astype(jnp.bfloat16), gate_acc.reshape(TOKENS, TOPK)
```

```python
import jax
import jax.numpy as jnp
from jax import lax
from jax.sharding import PartitionSpec as P

BOTH = ("expert", "tensor")
F32 = jnp.float32
BF16 = jnp.bfloat16


def silu_pair(pre_act):
    sigma = jax.nn.sigmoid(pre_act)
    return (pre_act * sigma, sigma * (1.0 + pre_act * (1.0 - sigma)))


def routed_local(grad_out, gate_weights, slot_lists, saved_gate, saved_up, w_gate, w_up, w_down):
    slot_table = slot_lists[0]
    experts, capacity = slot_table.shape
    tok_count, quarter = grad_out.shape
    top_count = gate_weights.shape[1]
    entries = slot_table.reshape(-1)
    occupied = entries >= 0
    owner_token = jnp.where(occupied, entries // top_count, -1)
    picker = owner_token[:, None] == jnp.arange(tok_count, dtype=jnp.int32)[None, :]
    picker_half = picker.astype(jnp.bfloat16)
    send_rows = jnp.dot(picker_half, grad_out, preferred_element_type=jnp.float32).astype(
        jnp.bfloat16
    )
    send_gate = jnp.where(
        occupied, gate_weights.reshape(-1)[jnp.maximum(entries, 0)], jnp.zeros((), jnp.bfloat16)
    )
    got_rows, got_gate = (
        lax.all_to_all(
            send_rows.reshape(experts, capacity, quarter),
            "expert",
            split_axis=0,
            concat_axis=0,
            tiled=True,
        ),
        lax.all_to_all(
            send_gate.reshape(experts, capacity), "expert", split_axis=0, concat_axis=0, tiled=True
        ),
    )
    slot_count = got_rows.shape[0] * capacity
    routed = got_rows.reshape(slot_count, quarter)
    down_proj = w_down[0]
    contract = (((1,), (1,)), ((), ()))
    back_hidden = lax.dot_general(
        lax.all_gather(routed, "tensor", axis=1, tiled=True),
        down_proj,
        contract,
        preferred_element_type=jnp.float32,
    )
    gate_pre = saved_gate[0].astype(jnp.float32)
    up_pre = saved_up[0].astype(jnp.float32)
    activated, derivative = silu_pair(gate_pre)
    hidden = activated * up_pre
    slot_gate_grad = lax.psum(jnp.sum(back_hidden * hidden, axis=1), "tensor")
    scaled = got_gate.reshape(slot_count).astype(jnp.float32)[:, None] * back_hidden
    grad_pre_gate = (scaled * up_pre * derivative).astype(jnp.bfloat16)
    grad_pre_up = (scaled * activated).astype(jnp.bfloat16)
    gate_proj = w_gate[0]
    up_proj = w_up[0]
    partial_rows = lax.dot_general(
        gate_proj, grad_pre_gate, contract, preferred_element_type=jnp.float32
    )
    partial_rows = (
        partial_rows
        + lax.dot_general(up_proj, grad_pre_up, contract, preferred_element_type=jnp.float32)
    ).astype(jnp.bfloat16)
    back_rows = lax.all_to_all(partial_rows, "expert", split_axis=1, concat_axis=1, tiled=True)
    back_gate = lax.all_to_all(
        slot_gate_grad.reshape(1, slot_count), "expert", split_axis=1, concat_axis=1, tiled=True
    )
    local_sums = lax.dot_general(
        picker_half, back_rows, (((0,), (1,)), ((), ())), preferred_element_type=jnp.float32
    )
    grad_in = lax.psum_scatter(
        local_sums.astype(jnp.bfloat16), "tensor", scatter_dimension=1, tiled=True
    )
    position = jnp.where(occupied, entries, tok_count * top_count)
    gate_sums = (
        jnp.zeros((tok_count * top_count + 1,), jnp.float32).at[position].add(back_gate.reshape(-1))
    )
    grad_gate = gate_sums[:-1].reshape(tok_count, top_count)
    return (grad_in, grad_gate)


NZ, NY, NX, NC = 4, 2, 2, 2


def _pairs(move):
    pairs = []
    for z in range(NZ):
        for y in range(NY):
            for x in range(NX):
                for c in range(NC):
                    tz, ty, tx, tc = move(z, y, x, c)
                    pairs.append((((z * NY + y) * NX + x) * NC + c, ((tz * NY + ty) * NX + tx) * NC + tc))
    return pairs


TO_X = _pairs(lambda z, y, x, c: (z, y, 1 - x, c))
TO_Y = _pairs(lambda z, y, x, c: (z, 1 - y, x, c))
TO_CORE = _pairs(lambda z, y, x, c: (z, y, x, 1 - c))
CORNER = _pairs(lambda z, y, x, c: (z, y, 1 - x, c) if c == 0 else (z, 1 - y, x, c))
Z_UP = [_pairs(lambda z, y, x, c, d=d: ((z + d) % NZ, y, x, c)) for d in range(NZ)]


def send(value, pairs):
    return lax.ppermute(value, BOTH, pairs)


def dot_nt(a, b):
    return lax.dot_general(a, b, (((1,), (1,)), ((), ())), preferred_element_type=F32)


def dense_local(grad_out, gate_weights, slot_lists, saved_gate, saved_up, w_gate, w_up, w_down):
    tokens, quarter = grad_out.shape
    experts = slot_lists.shape[1]
    top_count = gate_weights.shape[1]
    hid = saved_gate.shape[2]
    expert = lax.axis_index("expert")
    block = lax.axis_index("tensor")
    z, y = expert // NY, expert % NY
    x, c = block // NC, block % NC
    chunks = 2
    rows = tokens // chunks

    pieces = []
    for j in range(chunks):
        own = grad_out[j * rows : (j + 1) * rows]
        p00 = jnp.concatenate([own] + [send(own, Z_UP[d]) for d in range(1, NZ)], axis=0)
        p10 = send(p00, TO_Y)
        p01 = send(p00, TO_X)
        p11 = send(jnp.where(c == 0, p10, p01), CORNER)
        pieces.append(((p00, p01), (p10, p11)))

    entries = slot_lists[0]
    owner, choice = entries // top_count, entries % top_count
    token_ids = jnp.arange(tokens, dtype=jnp.int32)
    hit = owner[:, :, None] == token_ids[None, None, :]
    choice_of = jnp.sum(jnp.where(hit, choice[:, :, None], 0), axis=1)
    slot_of = jnp.sum(jnp.where(hit, token_ids[None, :, None], 0), axis=1)
    choice_ids = jnp.arange(top_count, dtype=jnp.int32)
    chosen = choice_of[:, :, None] == choice_ids[None, None, :]
    gate_of = jnp.sum(jnp.where(chosen, gate_weights[None].astype(F32), 0.0), axis=2)
    table = lax.all_gather(jnp.stack([slot_of.astype(F32), gate_of], axis=1), "expert", axis=0)
    table = lax.dynamic_index_in_dim(table, expert, axis=1, keepdims=False)

    def halves(w, axis):
        shape = w.shape[:axis] + (NX, NC, quarter) + w.shape[axis + 1 :]
        w = w.reshape(shape)
        keep = lax.dynamic_index_in_dim(w, c, axis=axis + 1, keepdims=False)
        give = lax.dynamic_index_in_dim(w, 1 - c, axis=axis + 1, keepdims=False)
        got = send(give, TO_CORE)

        def near(v, dx):
            return lax.dynamic_index_in_dim(v, jnp.where(dx == 0, x, 1 - x), axis=axis, keepdims=False)

        return [(near(keep, dx), near(got, dx)) for dx in range(NX)]

    down = halves(w_down[0], 1)
    gate_w = halves(w_gate[0], 0)
    up_w = halves(w_up[0], 0)

    factors = []
    sg = saved_gate[0].reshape(experts, tokens, hid)
    su = saved_up[0].reshape(experts, tokens, hid)
    for dy in range(NY):
        line = []
        for d in range(NZ):
            group = ((z + NZ - d) % NZ) * NY + (y if dy == 0 else 1 - y)
            slot_row = lax.dynamic_index_in_dim(table, group, axis=0, keepdims=False)
            pick = (slot_row[0].astype(jnp.int32)[:, None] == token_ids[None, :]).astype(BF16)
            gate_pre = jnp.dot(pick, lax.dynamic_index_in_dim(sg, group, 0, False), preferred_element_type=F32)
            up_pre = jnp.dot(pick, lax.dynamic_index_in_dim(su, group, 0, False), preferred_element_type=F32)
            activated, derivative = silu_pair(gate_pre)
            scale = slot_row[1][:, None]
            line.append((activated * up_pre, scale * up_pre * derivative, scale * activated))
        factors.append(line)

    gate_terms = []
    results = []
    for j in range(chunks):
        lo, hi = j * rows, (j + 1) * rows
        ready = []
        for dy in range(NY):
            (a, b) = pieces[j][dy]
            mine = dot_nt(a, down[0][0]) + dot_nt(b, down[1][0])
            theirs = dot_nt(a, down[0][1]) + dot_nt(b, down[1][1])
            ready.append((mine, theirs))
        back = send(jnp.concatenate([r[1] for r in ready], axis=0), TO_CORE)
        gp, up, terms = [], [], []
        for dy in range(NY):
            bh = ready[dy][0] + back[dy * NZ * rows : (dy + 1) * NZ * rows]
            f = [jnp.concatenate([factors[dy][d][i][lo:hi] for d in range(NZ)], axis=0) for i in range(3)]
            terms.append(jnp.sum(bh * f[0], axis=1))
            gp.append((bh * f[1]).astype(BF16))
            up.append((bh * f[2]).astype(BF16))
        gate_terms.append(jnp.stack(terms).reshape(NY, NZ, rows))
        mine = jnp.concatenate([jnp.concatenate(gp, 0), jnp.concatenate(up, 0)], axis=1)
        theirs = send(mine, TO_CORE)

        def grad(dy, dx):
            s = slice(dy * NZ * rows, (dy + 1) * NZ * rows)
            m, t = mine[s], theirs[s]
            return (
                dot_nt(m[:, :hid], gate_w[dx][0])
                + dot_nt(m[:, hid:], up_w[dx][0])
                + dot_nt(t[:, :hid], gate_w[dx][1])
                + dot_nt(t[:, hid:], up_w[dx][1])
            )

        r11 = send(grad(1, 1).astype(BF16), CORNER).astype(F32)
        r10 = (grad(1, 0) + jnp.where(c == 0, r11, 0.0)).astype(BF16)
        r01 = (grad(0, 1) + jnp.where(c == 0, 0.0, r11)).astype(BF16)
        r00 = grad(0, 0) + send(r10, TO_Y).astype(F32) + send(r01, TO_X).astype(F32)
        total = r00[:rows]
        for d in range(1, NZ):
            total = total + send(r00[d * rows : (d + 1) * rows].astype(BF16), Z_UP[NZ - d]).astype(F32)
        results.append(total.astype(BF16))
    grad_in = jnp.concatenate(results, axis=0)

    terms = jnp.concatenate(gate_terms, axis=2)
    everyone = lax.all_gather(terms, BOTH, axis=0)
    everyone = everyone.reshape(NZ, NY, NX * NC, NY, NZ, tokens)
    everyone = jnp.sum(everyone, axis=2)
    src_z = jnp.arange(NZ, dtype=jnp.int32)
    src_y = jnp.arange(NY, dtype=jnp.int32)
    want = ((src_z[:, None] - jnp.arange(NZ)[None, :]) % NZ == z)[:, None, None, :]
    want = want & ((src_y[:, None] ^ src_y[None, :]) == y)[None, :, :, None]
    slot_grad = jnp.sum(jnp.where(want[..., None], everyone, 0.0), axis=(2, 3)).reshape(experts, tokens)
    grad_gate = jnp.sum(jnp.where(chosen, slot_grad[:, :, None], 0.0), axis=0)
    return (grad_in, grad_gate)


def local(grad_out, gate_weights, slot_lists, *rest):
    tokens = grad_out.shape[0]
    _, experts, capacity = slot_lists.shape
    dense = experts == gate_weights.shape[1] == NZ * NY and capacity == tokens
    dense = dense and lax.axis_size("expert") == NZ * NY and lax.axis_size("tensor") == NX * NC
    program = dense_local if dense else routed_local
    return program(grad_out, gate_weights, slot_lists, *rest)


def solution(mesh):
    in_specs = (
        P("expert", "tensor"),
        P("expert", None),
        P("expert", None, None),
        P("expert", None, "tensor"),
        P("expert", None, "tensor"),
        P("expert", None, "tensor"),
        P("expert", None, "tensor"),
        P("expert", "tensor", None),
    )
    out_specs = (P("expert", "tensor"), P("expert", None))
    return jax.shard_map(local, mesh=mesh, in_specs=in_specs, out_specs=out_specs, check_vma=False)
```

```python
import jax
import jax.numpy as jnp
from jax import lax
from jax.experimental import pallas as pl
from jax.experimental.pallas import tpu as pltpu
from jax.sharding import PartitionSpec as P

BOTH = ("expert", "tensor")
F32 = jnp.float32
BF16 = jnp.bfloat16


def silu_pair(pre_act):
    sigma = jax.nn.sigmoid(pre_act)
    return (pre_act * sigma, sigma * (1.0 + pre_act * (1.0 - sigma)))


def routed_local(grad_out, gate_weights, slot_lists, saved_gate, saved_up, w_gate, w_up, w_down):
    slot_table = slot_lists[0]
    experts, capacity = slot_table.shape
    tok_count, quarter = grad_out.shape
    top_count = gate_weights.shape[1]
    entries = slot_table.reshape(-1)
    occupied = entries >= 0
    owner_token = jnp.where(occupied, entries // top_count, -1)
    picker = owner_token[:, None] == jnp.arange(tok_count, dtype=jnp.int32)[None, :]
    picker_half = picker.astype(jnp.bfloat16)
    send_rows = jnp.dot(picker_half, grad_out, preferred_element_type=jnp.float32).astype(
        jnp.bfloat16
    )
    send_gate = jnp.where(
        occupied, gate_weights.reshape(-1)[jnp.maximum(entries, 0)], jnp.zeros((), jnp.bfloat16)
    )
    got_rows, got_gate = (
        lax.all_to_all(
            send_rows.reshape(experts, capacity, quarter),
            "expert",
            split_axis=0,
            concat_axis=0,
            tiled=True,
        ),
        lax.all_to_all(
            send_gate.reshape(experts, capacity), "expert", split_axis=0, concat_axis=0, tiled=True
        ),
    )
    slot_count = got_rows.shape[0] * capacity
    routed = got_rows.reshape(slot_count, quarter)
    down_proj = w_down[0]
    contract = (((1,), (1,)), ((), ()))
    back_hidden = lax.dot_general(
        lax.all_gather(routed, "tensor", axis=1, tiled=True),
        down_proj,
        contract,
        preferred_element_type=jnp.float32,
    )
    gate_pre = saved_gate[0].astype(jnp.float32)
    up_pre = saved_up[0].astype(jnp.float32)
    activated, derivative = silu_pair(gate_pre)
    hidden = activated * up_pre
    slot_gate_grad = lax.psum(jnp.sum(back_hidden * hidden, axis=1), "tensor")
    scaled = got_gate.reshape(slot_count).astype(jnp.float32)[:, None] * back_hidden
    grad_pre_gate = (scaled * up_pre * derivative).astype(jnp.bfloat16)
    grad_pre_up = (scaled * activated).astype(jnp.bfloat16)
    gate_proj = w_gate[0]
    up_proj = w_up[0]
    partial_rows = lax.dot_general(
        gate_proj, grad_pre_gate, contract, preferred_element_type=jnp.float32
    )
    partial_rows = (
        partial_rows
        + lax.dot_general(up_proj, grad_pre_up, contract, preferred_element_type=jnp.float32)
    ).astype(jnp.bfloat16)
    back_rows = lax.all_to_all(partial_rows, "expert", split_axis=1, concat_axis=1, tiled=True)
    back_gate = lax.all_to_all(
        slot_gate_grad.reshape(1, slot_count), "expert", split_axis=1, concat_axis=1, tiled=True
    )
    local_sums = lax.dot_general(
        picker_half, back_rows, (((0,), (1,)), ((), ())), preferred_element_type=jnp.float32
    )
    grad_in = lax.psum_scatter(
        local_sums.astype(jnp.bfloat16), "tensor", scatter_dimension=1, tiled=True
    )
    position = jnp.where(occupied, entries, tok_count * top_count)
    gate_sums = (
        jnp.zeros((tok_count * top_count + 1,), jnp.float32).at[position].add(back_gate.reshape(-1))
    )
    grad_gate = gate_sums[:-1].reshape(tok_count, top_count)
    return (grad_in, grad_gate)


NZ, NY, NX, NC = 4, 2, 2, 2


def _pairs(move):
    pairs = []
    for z in range(NZ):
        for y in range(NY):
            for x in range(NX):
                for c in range(NC):
                    tz, ty, tx, tc = move(z, y, x, c)
                    pairs.append((((z * NY + y) * NX + x) * NC + c, ((tz * NY + ty) * NX + tx) * NC + tc))
    return pairs


TO_X = _pairs(lambda z, y, x, c: (z, y, 1 - x, c))
TO_Y = _pairs(lambda z, y, x, c: (z, 1 - y, x, c))
TO_CORE = _pairs(lambda z, y, x, c: (z, y, x, 1 - c))
LEFT = _pairs(lambda z, y, x, c: (z, y, 1 - x, c) if c == 0 else (z, 1 - y, x, c))
RIGHT = _pairs(lambda z, y, x, c: (z, 1 - y, x, c) if c == 0 else (z, y, 1 - x, c))
TO_Z = [_pairs(lambda z, y, x, c, d=d: (z ^ d, y, x, c)) for d in range(NZ)]
CHUNKS = ((0, 2), (1, 3))


def send(value, pairs, name="send"):
    with jax.named_scope(name):
        return lax.ppermute(value, BOTH, pairs)


def after(value, *first):
    return lax.optimization_barrier((value, *first))[0]


def dot_nt(a, b):
    return lax.dot_general(a, b, (((1,), (1,)), ((), ())), preferred_element_type=F32)


def shape_of(shape, dtype):
    return jax.ShapeDtypeStruct(shape, dtype)


HINT = pl.CostEstimate(flops=0, transcendentals=0, bytes_accessed=0)
LARGE = pltpu.CompilerParams(vmem_limit_bytes=48 << 20)


def kernel(name, body, outs, grid, in_specs, out_specs, *args, scratch=()):
    return pl.pallas_call(
        body,
        out_shape=outs,
        grid_spec=pltpu.PrefetchScalarGridSpec(
            num_scalar_prefetch=1, grid=grid, in_specs=in_specs, out_specs=out_specs, scratch_shapes=scratch
        ),
        compiler_params=LARGE,
        cost_estimate=HINT,
        name=name,
    )(*args)


def prepare(expert, table, saved_gate, saved_up):
    groups, _, tokens = table.shape
    hid = saved_gate.shape[1]

    def spot(i):
        return (i // 2) % NY, i // 4 + 2 * (i % 2)

    def group(i, s):
        dy, d = spot(i)
        return ((s[0] // NY) ^ d) * NY + ((s[0] % NY) ^ dy)

    def body(s_ref, t_ref, g_ref, u_ref, *outs):
        slots = lax.broadcasted_iota(jnp.int32, (tokens, tokens), 0).astype(F32)
        pick = jnp.where(slots == t_ref[0, 0:1, :], 1.0, 0.0).astype(BF16)
        flip = (((0,), (0,)), ((), ()))
        gate_pre = lax.dot_general(pick, g_ref[...], flip, preferred_element_type=F32)
        up_pre = lax.dot_general(pick, u_ref[...], flip, preferred_element_type=F32)
        scale = jnp.transpose(jnp.broadcast_to(t_ref[0, 1:2, :], (tokens, tokens)))[:, 0:1]
        activated, derivative = silu_pair(gate_pre)
        outs[0][...] = activated * up_pre
        outs[1][...] = scale * up_pre * derivative
        outs[2][...] = scale * activated

    out = shape_of((groups * tokens, hid), F32)
    saved = pl.BlockSpec((tokens, hid), lambda i, s: (group(i, s), 0))
    row = pl.BlockSpec((1, 2, tokens), lambda i, s: (spot(i)[0] * NZ + spot(i)[1], 0, 0))
    spec = pl.BlockSpec((tokens, hid), lambda i, s: (i, 0))
    return kernel(
        "prepare", body, [out] * 3, (groups,), [row, saved, saved], [spec] * 3, expert, table, saved_gate, saved_up
    )


def hidden_parts(block, pieces, down, got):
    tokens, quarter = pieces[0][0].shape
    hid = down.shape[0]
    count = len(pieces)
    half = count * tokens
    rows = NY * half

    def body(s_ref, *refs):
        near = refs[: 4 * count]
        d_ref, o_ref, mine, theirs, rows_v, w_v, row_sem, w_sem = refs[4 * count :]
        x, c = s_ref[0] // NC, s_ref[0] % NC

        def columns(q):
            return pl.ds(pl.multiple_of(q * quarter, quarter), quarter)

        def weight(dx, k):
            source = (d_ref, o_ref)[k].at[:, columns(2 * (x ^ dx) + c)]
            return pltpu.make_async_copy(source, w_v.at[dx, k], w_sem.at[dx, k])

        def piece(i, j, dx, dy):
            target = rows_v.at[dx, pl.ds(dy * half + i * tokens, tokens), :]
            return pltpu.make_async_copy(near[4 * i + j], target, row_sem.at[i, dx, dy])

        for dx in range(NX):
            for k in (1, 0):
                weight(dx, k).start()
            for i in range(count):
                piece(i, 0 if dx == 0 else 3, dx, dx).start()

                @pl.when(c == dx)
                def _(i=i, dx=dx):
                    piece(i, 1, dx, 1 - dx).start()

                @pl.when(c != dx)
                def _(i=i, dx=dx):
                    piece(i, 2, dx, 1 - dx).start()

        total = [None, None]
        for dx in range(NX):
            for i in range(count):
                for dy in range(NY):
                    piece(i, 0, dx, dy).wait()
            for k in (1, 0):
                weight(dx, k).wait()
                part = dot_nt(rows_v[dx], w_v[dx, k])
                total[k] = part if dx == 0 else total[k] + part
        theirs[...] = total[1].astype(BF16)
        mine[...] = total[0]

    flat = [p for four in pieces for p in four]
    spec = lambda cols: pl.BlockSpec((rows, cols), lambda i, s: (0, 0))
    return kernel(
        "hidden",
        body,
        [shape_of((rows, hid), F32), shape_of((rows, hid), BF16)],
        (1,),
        [pl.BlockSpec(memory_space=pl.ANY)] * (len(flat) + 2),
        [spec(hid)] * 2,
        block,
        *flat,
        down,
        got,
        scratch=[
            pltpu.VMEM((NX, rows, quarter), BF16),
            pltpu.VMEM((NX, 2, hid, quarter), BF16),
            pltpu.SemaphoreType.DMA((count, NX, NY)),
            pltpu.SemaphoreType.DMA((NX, 2)),
        ],
    )


def pre_grads(block, mine, back, factors, number):
    rows, hid = mine.shape
    half = rows // NY
    tokens = factors[0].shape[0] // (NY * NZ)
    count = half // tokens

    def body(s_ref, m_ref, b_ref, f0, f1, f2, h_ref, t_ref):
        bh = m_ref[...] + b_ref[...].astype(F32)
        h_ref[:, :hid] = (bh * f1[...]).astype(BF16)
        h_ref[:, hid:] = (bh * f2[...]).astype(BF16)
        term = jnp.sum(bh * f0[...], axis=1, keepdims=True)
        flat = jnp.transpose(jnp.broadcast_to(term, (half, 128)))
        for i in range(count):
            t_ref[0, i : i + 1, :] = flat[0:1, i * tokens : (i + 1) * tokens]

    outs = [shape_of((rows, 2 * hid), BF16), shape_of((NY, count, tokens), F32)]
    spec = lambda cols, first=0: pl.BlockSpec((half, cols), lambda i, s: (first + i, 0))
    return kernel(
        "pre_grads",
        body,
        outs,
        (NY,),
        [spec(hid)] * 2 + [spec(hid, NY * number)] * 3,
        [spec(2 * hid), pl.BlockSpec((1, count, tokens), lambda i, s: (i, 0, 0))],
        block,
        mine,
        back,
        *factors,
    )


def input_parts(block, mine, theirs, weights, got, spots, types):
    rows = mine.shape[0] // NY
    hid = mine.shape[1] // 2
    quarter = weights[0].shape[0] // (NX * NC)
    steps = 2
    wide = quarter // steps

    def place(i, s):
        c = s[0] % NC
        pairs = [spot(c) for spot in spots]
        dy = jnp.where(i == 0, pairs[0][0], pairs[1][0])
        dx = jnp.where(i == 0, pairs[0][1], pairs[1][1])
        return dy, 2 * ((s[0] // NC) ^ dx) + c

    def body(s_ref, m_ref, t_ref, wg, wu, og, ou, *outs):
        total = dot_nt(m_ref[:, :hid], wg[...]) + dot_nt(m_ref[:, hid:], wu[...])
        total = total + dot_nt(t_ref[:, :hid], og[...]) + dot_nt(t_ref[:, hid:], ou[...])
        for k, out in enumerate(outs):

            @pl.when(pl.program_id(0) == k)
            def _(out=out):
                out[...] = total.astype(out.dtype)

    half = pl.BlockSpec((rows, 2 * hid), lambda i, j, s: (place(i, s)[0], 0))
    weight = pl.BlockSpec((wide, hid), lambda i, j, s: (place(i, s)[1] * steps + j, 0))
    outs = [
        pl.BlockSpec((rows, wide), lambda i, j, s: (0, jnp.where(i == 0, j, steps - 1))),
        pl.BlockSpec((rows, wide), lambda i, j, s: (0, jnp.where(i == 0, 0, j))),
    ]
    return kernel(
        "input",
        body,
        [shape_of((rows, quarter), t) for t in types],
        (2, steps),
        [half, half] + [weight] * 4,
        outs,
        block,
        mine,
        theirs,
        *weights,
        *got,
    )


def add_pieces(block, base, first, second, types):
    rows, cols = base.shape
    part = rows // len(types)
    wide = cols // 2

    def body(s_ref, b_ref, f_ref, g_ref, *outs):
        for i, out in enumerate(outs):
            s = slice(i * part, (i + 1) * part)
            out[...] = (b_ref[s] + f_ref[s].astype(F32) + g_ref[s].astype(F32)).astype(out.dtype)

    spec = lambda n: pl.BlockSpec((n, wide), lambda i, s: (0, i))
    outs = [shape_of((part, cols), t) for t in types]
    return kernel("add", body, outs, (2,), [spec(rows)] * 3, [spec(part)] * len(outs), block, base, first, second)


def add_corner(block, base, corner):
    rows, cols = base.shape

    def body(s_ref, b_ref, c_ref, out):
        out[...] = (b_ref[...].astype(F32) + c_ref[...].astype(F32)).astype(BF16)

    spec = pl.BlockSpec((rows, cols // 2), lambda i, s: (0, i))
    return kernel("corner", body, shape_of(base.shape, BF16), (2,), [spec] * 2, spec, block, base, corner)


def last_sum(block, keep, parts):
    def body(s_ref, k_ref, *refs):
        total = k_ref[...]
        for ref in refs[:-1]:
            total = total + ref[...].astype(F32)
        refs[-1][...] = total.astype(BF16)

    spec = pl.BlockSpec(keep.shape, lambda i, s: (0, 0))
    return kernel(
        "last", body, shape_of(keep.shape, BF16), (1,), [spec] * (1 + len(parts)), spec, block, keep, *parts
    )


def dense_local(grad_out, gate_weights, slot_lists, saved_gate, saved_up, w_gate, w_up, w_down):
    tokens, quarter = grad_out.shape
    experts = slot_lists.shape[1]
    top_count = gate_weights.shape[1]
    expert = lax.axis_index("expert")
    block = lax.axis_index("tensor")
    z, y = expert // NY, expert % NY
    at_expert, at_block = expert.reshape(1), block.reshape(1)

    down, gate_w, up_w = w_down[0], w_gate[0], w_up[0]

    entries = slot_lists[0]
    owner, choice = entries // top_count, entries % top_count
    token_ids = jnp.arange(tokens, dtype=jnp.int32)
    hit = owner[:, :, None] == token_ids[None, None, :]
    choice_of = jnp.sum(jnp.where(hit, choice[:, :, None], 0), axis=1)
    slot_of = jnp.sum(jnp.where(hit, token_ids[None, :, None], 0), axis=1)
    choice_ids = jnp.arange(top_count, dtype=jnp.int32)
    chosen = choice_of[:, :, None] == choice_ids[None, None, :]
    gate_of = jnp.sum(jnp.where(chosen, gate_weights[None].astype(F32), 0.0), axis=2)
    table = jnp.stack([slot_of.astype(F32), gate_of], axis=1).reshape(NZ, NY, 2, tokens)

    own = grad_out
    z2, z1 = send(own, TO_Z[2], "z2"), send(own, TO_Z[1], "z1")
    first0, second0 = send(own, RIGHT, "first0"), send(own, LEFT, "second0")
    got_down = send(down, TO_CORE, "weights")

    own_, z2, z1, first0, second0, got_down, table = lax.optimization_barrier(
        (own, z2, z1, first0, second0, got_down, table)
    )
    z3 = send(own_, TO_Z[3], "z3")
    first2, second2 = send(z2, RIGHT, "first2"), send(z2, LEFT, "second2")
    third0 = send(first0, LEFT, "third0")
    line = []
    for d in range(NZ):
        part = lax.dynamic_index_in_dim(table, z ^ d, axis=0, keepdims=False)
        line.append(part if d == 0 else send(part, TO_Z[d], "meta"))
    line = jnp.stack(line)
    gate_w_, up_w_ = after(gate_w, table), after(up_w, table)
    got_gate, got_up = send(gate_w_, TO_CORE, "weights"), send(up_w_, TO_CORE, "weights")

    z1, z3, first2, second2, third0, line, got_gate, got_up = lax.optimization_barrier(
        (z1, z3, first2, second2, third0, line, got_gate, got_up)
    )
    first1, second1 = send(z1, RIGHT, "first1"), send(z1, LEFT, "second1")
    third2 = send(first2, LEFT, "third2")
    near = lax.dynamic_index_in_dim(line, y, axis=1, keepdims=False)
    far = send(lax.dynamic_index_in_dim(line, 1 - y, axis=1, keepdims=False), TO_Y, "meta_y")
    table = jnp.concatenate([near, far], axis=0)

    z3, first1, second1, third2, table = lax.optimization_barrier((z3, first1, second1, third2, table))
    first3, second3 = send(z3, RIGHT, "first3"), send(z3, LEFT, "second3")
    third1 = send(first1, LEFT, "third1")
    factors = prepare(at_expert, table, saved_gate[0], saved_up[0])

    pieces = {0: (own, first0, second0, third0), 2: (z2, first2, second2, third2)}

    weights, got = (gate_w, up_w), (got_gate, got_up)
    near, far = CHUNKS

    def stage_hidden(place, chunk):
        mine, theirs = hidden_parts(place, [pieces[d] for d in chunk], down, got_down)
        return mine, send(theirs, TO_CORE, f"swap_bh{chunk[0]}"), after(at_block, mine)

    def stage_pre(place, chunk, mine, back):
        mine, term = pre_grads(place, mine, back, factors, CHUNKS.index(chunk))
        return mine, send(mine, TO_CORE, f"swap_h{chunk[0]}"), term, after(at_block, mine)

    def stage_out(place, chunk, mine, theirs):
        a, b = input_parts(
            place, mine, theirs, weights, got, (lambda c: (1, 1), lambda c: (c, 1 - c)), (BF16, BF16)
        )
        corner = send(a, LEFT, f"r_corner{chunk[0]}")
        right = send(b, LEFT, f"r_right{chunk[0]}")
        return corner, right, after(at_block, a)

    def stage_keep(place, mine, theirs):
        base, left = input_parts(
            place, mine, theirs, weights, got, (lambda c: (0, 0), lambda c: (1 - c, c)), (F32, BF16)
        )
        return base, left, after(at_block, base)

    def stage_corner(place, chunk, left, corner):
        value = add_corner(place, left, corner)
        return send(value, RIGHT, f"r_left{chunk[0]}"), after(at_block, value)

    def stage_add(place, chunk, base, right, left):
        types = [F32 if d == 0 else BF16 for d in chunk]
        totals = add_pieces(place, base, right, left, types)
        sums = {d: t if d == 0 else send(t, TO_Z[d], f"r_z{d}") for d, t in zip(chunk, totals)}
        return sums, after(at_block, totals[0])

    place = after(at_block, factors[0])
    mine_a, back, place = stage_hidden(place, near)
    mine_a, theirs_a, term_a, place = stage_pre(place, near, mine_a, back)
    theirs_a, first3, second3, third1 = lax.optimization_barrier((theirs_a, first3, second3, third1))
    third3 = send(first3, LEFT, "third3")
    pieces |= {1: (z1, first1, second1, third1), 3: (z3, first3, second3, third3)}
    corner_a, right_a, place = stage_out(place, near, mine_a, theirs_a)
    base_a, left_a, place = stage_keep(place, mine_a, theirs_a)
    mine_b, back, place = stage_hidden(place, far)
    left_a, place = stage_corner(place, near, left_a, corner_a)
    mine_b, theirs_b, term_b, place = stage_pre(place, far, mine_b, back)
    corner_b, right_b, place = stage_out(place, far, mine_b, theirs_b)
    base_b, left_b, place = stage_keep(place, mine_b, theirs_b)
    sums, place = stage_add(place, near, base_a, right_a, left_a)
    left_b, place = stage_corner(place, far, left_b, corner_b)
    more, place = stage_add(place, far, base_b, right_b, left_b)
    sums.update(more)
    grad_in = last_sum(place, sums[0], [sums[d] for d in (2, 1, 3)])

    terms = {d: t[:, i] for c, t in ((near, term_a), (far, term_b)) for i, d in enumerate(c)}
    term = jnp.stack([terms[d] for d in range(NZ)], axis=1)
    term = term + send(term, TO_CORE, "t_core")
    term = term + send(term, TO_X, "t_x")
    term = jnp.stack([term[0], send(term[1], TO_Y, "t_y")], axis=1)
    slots = [term[0]] + [send(term[d], TO_Z[d], f"t_z{d}") for d in range(1, NZ)]
    slot_grad = jnp.zeros((experts, tokens), F32)
    ids = jnp.arange(experts, dtype=jnp.int32)
    for d in range(NZ):
        for dy in range(NY):
            source = (z ^ d) * NY + (y ^ dy)
            slot_grad = jnp.where((ids == source)[:, None], slots[d][dy][None], slot_grad)
    grad_gate = jnp.sum(jnp.where(chosen, slot_grad[:, :, None], 0.0), axis=0)
    return (grad_in, grad_gate)


def local(grad_out, gate_weights, slot_lists, *rest):
    tokens = grad_out.shape[0]
    _, experts, capacity = slot_lists.shape
    dense = experts == gate_weights.shape[1] == NZ * NY and capacity == tokens
    dense = dense and lax.axis_size("expert") == NZ * NY and lax.axis_size("tensor") == NX * NC
    program = dense_local if dense else routed_local
    return program(grad_out, gate_weights, slot_lists, *rest)


def solution(mesh):
    in_specs = (
        P("expert", "tensor"),
        P("expert", None),
        P("expert", None, None),
        P("expert", None, "tensor"),
        P("expert", None, "tensor"),
        P("expert", None, "tensor"),
        P("expert", None, "tensor"),
        P("expert", "tensor", None),
    )
    out_specs = (P("expert", "tensor"), P("expert", None))
    return jax.shard_map(local, mesh=mesh, in_specs=in_specs, out_specs=out_specs, check_vma=False)
```

```python
import jax
import jax.numpy as jnp
from jax import lax
from jax.experimental import pallas as pl
from jax.experimental.pallas import tpu as pltpu
from jax.sharding import PartitionSpec as P

BOTH = ("expert", "tensor")
F32 = jnp.float32
BF16 = jnp.bfloat16


def silu_pair(pre_act):
    sigma = jax.nn.sigmoid(pre_act)
    return (pre_act * sigma, sigma * (1.0 + pre_act * (1.0 - sigma)))


def routed_local(grad_out, gate_weights, slot_lists, saved_gate, saved_up, w_gate, w_up, w_down):
    slot_table = slot_lists[0]
    experts, capacity = slot_table.shape
    tok_count, quarter = grad_out.shape
    top_count = gate_weights.shape[1]
    entries = slot_table.reshape(-1)
    occupied = entries >= 0
    owner_token = jnp.where(occupied, entries // top_count, -1)
    picker = owner_token[:, None] == jnp.arange(tok_count, dtype=jnp.int32)[None, :]
    picker_half = picker.astype(jnp.bfloat16)
    send_rows = jnp.dot(picker_half, grad_out, preferred_element_type=jnp.float32).astype(
        jnp.bfloat16
    )
    send_gate = jnp.where(
        occupied, gate_weights.reshape(-1)[jnp.maximum(entries, 0)], jnp.zeros((), jnp.bfloat16)
    )
    got_rows, got_gate = (
        lax.all_to_all(
            send_rows.reshape(experts, capacity, quarter),
            "expert",
            split_axis=0,
            concat_axis=0,
            tiled=True,
        ),
        lax.all_to_all(
            send_gate.reshape(experts, capacity), "expert", split_axis=0, concat_axis=0, tiled=True
        ),
    )
    slot_count = got_rows.shape[0] * capacity
    routed = got_rows.reshape(slot_count, quarter)
    down_proj = w_down[0]
    contract = (((1,), (1,)), ((), ()))
    back_hidden = lax.dot_general(
        lax.all_gather(routed, "tensor", axis=1, tiled=True),
        down_proj,
        contract,
        preferred_element_type=jnp.float32,
    )
    gate_pre = saved_gate[0].astype(jnp.float32)
    up_pre = saved_up[0].astype(jnp.float32)
    activated, derivative = silu_pair(gate_pre)
    hidden = activated * up_pre
    slot_gate_grad = lax.psum(jnp.sum(back_hidden * hidden, axis=1), "tensor")
    scaled = got_gate.reshape(slot_count).astype(jnp.float32)[:, None] * back_hidden
    grad_pre_gate = (scaled * up_pre * derivative).astype(jnp.bfloat16)
    grad_pre_up = (scaled * activated).astype(jnp.bfloat16)
    gate_proj = w_gate[0]
    up_proj = w_up[0]
    partial_rows = lax.dot_general(
        gate_proj, grad_pre_gate, contract, preferred_element_type=jnp.float32
    )
    partial_rows = (
        partial_rows
        + lax.dot_general(up_proj, grad_pre_up, contract, preferred_element_type=jnp.float32)
    ).astype(jnp.bfloat16)
    back_rows = lax.all_to_all(partial_rows, "expert", split_axis=1, concat_axis=1, tiled=True)
    back_gate = lax.all_to_all(
        slot_gate_grad.reshape(1, slot_count), "expert", split_axis=1, concat_axis=1, tiled=True
    )
    local_sums = lax.dot_general(
        picker_half, back_rows, (((0,), (1,)), ((), ())), preferred_element_type=jnp.float32
    )
    grad_in = lax.psum_scatter(
        local_sums.astype(jnp.bfloat16), "tensor", scatter_dimension=1, tiled=True
    )
    position = jnp.where(occupied, entries, tok_count * top_count)
    gate_sums = (
        jnp.zeros((tok_count * top_count + 1,), jnp.float32).at[position].add(back_gate.reshape(-1))
    )
    grad_gate = gate_sums[:-1].reshape(tok_count, top_count)
    return (grad_in, grad_gate)


NZ, NY, NX, NC = 4, 2, 2, 2


def _pairs(move):
    pairs = []
    for z in range(NZ):
        for y in range(NY):
            for x in range(NX):
                for c in range(NC):
                    tz, ty, tx, tc = move(z, y, x, c)
                    pairs.append((((z * NY + y) * NX + x) * NC + c, ((tz * NY + ty) * NX + tx) * NC + tc))
    return pairs


TO_X = _pairs(lambda z, y, x, c: (z, y, 1 - x, c))
TO_Y = _pairs(lambda z, y, x, c: (z, 1 - y, x, c))
TO_CORE = _pairs(lambda z, y, x, c: (z, y, x, 1 - c))
LEFT = _pairs(lambda z, y, x, c: (z, y, 1 - x, c) if c == 0 else (z, 1 - y, x, c))
RIGHT = _pairs(lambda z, y, x, c: (z, 1 - y, x, c) if c == 0 else (z, y, 1 - x, c))
TO_Z = [_pairs(lambda z, y, x, c, d=d: (z ^ d, y, x, c)) for d in range(NZ)]
CHUNKS = ((0, 2), (1, 3))


def send(value, pairs, name="send"):
    with jax.named_scope(name):
        return lax.ppermute(value, BOTH, pairs)


def after(value, *first):
    return lax.optimization_barrier((value, *first))[0]


def dot_nt(a, b):
    return lax.dot_general(a, b, (((1,), (1,)), ((), ())), preferred_element_type=F32)


def shape_of(shape, dtype):
    return jax.ShapeDtypeStruct(shape, dtype)


HINT = pl.CostEstimate(flops=0, transcendentals=0, bytes_accessed=0)
LARGE = pltpu.CompilerParams(vmem_limit_bytes=48 << 20)


def kernel(name, body, outs, grid, in_specs, out_specs, *args, scratch=()):
    return pl.pallas_call(
        body,
        out_shape=outs,
        grid_spec=pltpu.PrefetchScalarGridSpec(
            num_scalar_prefetch=1, grid=grid, in_specs=in_specs, out_specs=out_specs, scratch_shapes=scratch
        ),
        compiler_params=LARGE,
        cost_estimate=HINT,
        name=name,
    )(*args)


META = 8


def pack_rows(grad_out, slots, gates):
    tokens, quarter = grad_out.shape
    experts = slots.shape[0]
    top_count = gates.shape[0]

    def body(g_ref, s_ref, w_ref, out, choice_ref):
        out[:tokens] = g_ref[...]
        entries = s_ref[...]
        owner = lax.div(entries, top_count)
        choice = (entries - owner * top_count).astype(F32)
        owner = owner.astype(F32)
        gate = w_ref[...].astype(F32)
        square = lax.broadcasted_iota(jnp.int32, (tokens, tokens), 0).astype(F32)
        row = lax.broadcasted_iota(jnp.int32, (META, tokens), 0)
        lane = lax.broadcasted_iota(jnp.int32, (META, tokens), 1).astype(F32)
        number = lax.broadcasted_iota(jnp.int32, (top_count, tokens), 0).astype(F32)
        for e in range(experts):
            hit = jnp.where(square == owner[e : e + 1], 1.0, 0.0).astype(BF16)
            value = jnp.where(row == 0, lane, choice[e : e + 1]).astype(BF16)
            found = dot_nt(value, hit)
            chosen = found[1:2]
            weight = jnp.sum(jnp.where(number == chosen, gate, 0.0), axis=0, keepdims=True)
            choice_ref[e : e + 1, :] = chosen
            out[tokens:, e * tokens : (e + 1) * tokens] = jnp.where(row == 0, found, weight).astype(BF16)

    full = lambda shape: pl.BlockSpec(shape, lambda i: (0, 0))
    return pl.pallas_call(
        body,
        out_shape=[shape_of((tokens + META, quarter), BF16), shape_of((experts, tokens), F32)],
        grid=(1,),
        in_specs=[full(grad_out.shape), full(slots.shape), full(gates.shape)],
        out_specs=[full((tokens + META, quarter)), full((experts, tokens))],
        compiler_params=pltpu.CompilerParams(vmem_limit_bytes=60 << 20),
        cost_estimate=HINT,
        name="pack",
    )(grad_out, slots, gates)


def prepare(expert, block, near, saved_gate, saved_up, chunk):
    tokens = near[0][0].shape[0] - META
    hid = saved_gate.shape[1]
    count = len(chunk)
    low, step = chunk[0], chunk[1] - chunk[0]

    def group(i, e, s):
        return ((e[0] // NY) ^ (low + step * (i % count))) * NY + ((e[0] % NY) ^ (i // count))

    def body(e_ref, s_ref, *refs):
        metas = refs[: 3 * count]
        g_ref, u_ref = refs[3 * count : 3 * count + 2]
        outs = refs[3 * count + 2 :]
        i, c = pl.program_id(0), s_ref[0] % NC
        meta = None
        for k in range(count):
            own, first, second = (m[...].astype(F32) for m in metas[3 * k : 3 * k + 3])
            mine = jnp.where(i // count == 0, own, jnp.where(c == 0, first, second))
            meta = mine if meta is None else jnp.where(i % count == k, mine, meta)
        slots = lax.broadcasted_iota(jnp.int32, (tokens, tokens), 0).astype(F32)
        pick = jnp.where(slots == meta[0:1], 1.0, 0.0).astype(BF16)
        flip = (((0,), (0,)), ((), ()))
        gate_pre = lax.dot_general(pick, g_ref[...], flip, preferred_element_type=F32)
        up_pre = lax.dot_general(pick, u_ref[...], flip, preferred_element_type=F32)
        scale = jnp.transpose(jnp.broadcast_to(meta[1:2], (tokens, tokens)))[:, 0:1]
        activated, derivative = silu_pair(gate_pre)
        outs[0][...] = activated * up_pre
        outs[1][...] = scale * up_pre * derivative
        outs[2][...] = scale * activated

    out = shape_of((NY * count * tokens, hid), F32)
    meta = pl.BlockSpec((META, tokens), lambda i, e, s: (tokens // META, e[0]))
    saved = pl.BlockSpec((tokens, hid), lambda i, e, s: (group(i, e, s), 0))
    spec = pl.BlockSpec((tokens, hid), lambda i, e, s: (i, 0))
    flat = [p for three in near for p in three]
    return pl.pallas_call(
        body,
        out_shape=[out] * 3,
        grid_spec=pltpu.PrefetchScalarGridSpec(
            num_scalar_prefetch=2,
            grid=(NY * count,),
            in_specs=[meta] * len(flat) + [saved, saved],
            out_specs=[spec] * 3,
        ),
        compiler_params=LARGE,
        cost_estimate=HINT,
        name="prepare",
    )(expert, block, *flat, saved_gate, saved_up)


def hidden_parts(block, pieces, down, got):
    tokens, quarter = pieces[0][0].shape[0] - META, pieces[0][0].shape[1]
    hid = down.shape[0]
    count = len(pieces)
    half = count * tokens
    rows = NY * half

    def body(s_ref, *refs):
        near = refs[: 4 * count]
        d_ref, o_ref, mine, theirs, rows_v, w_v, row_sem, w_sem = refs[4 * count :]
        x, c = s_ref[0] // NC, s_ref[0] % NC

        def columns(q):
            return pl.ds(pl.multiple_of(q * quarter, quarter), quarter)

        def weight(dx, k):
            source = (d_ref, o_ref)[k].at[:, columns(2 * (x ^ dx) + c)]
            return pltpu.make_async_copy(source, w_v.at[dx, k], w_sem.at[dx, k])

        def piece(i, j, dx, dy):
            target = rows_v.at[dx, pl.ds(dy * half + i * tokens, tokens), :]
            source = near[4 * i + j].at[pl.ds(0, tokens), :]
            return pltpu.make_async_copy(source, target, row_sem.at[i, dx, dy])

        def begin(dx):
            for k in (1, 0):
                weight(dx, k).start()
            for i in range(count):
                piece(i, 0 if dx == 0 else 3, dx, dx).start()

                @pl.when(c == dx)
                def _(i=i, dx=dx):
                    piece(i, 1, dx, 1 - dx).start()

                @pl.when(c != dx)
                def _(i=i, dx=dx):
                    piece(i, 2, dx, 1 - dx).start()

        total = [None, None]
        begin(0)
        for dx in range(NX):
            for i in range(count):
                for dy in range(NY):
                    piece(i, 0, dx, dy).wait()
            for k in (1, 0):
                weight(dx, k).wait()
            if dx + 1 < NX:
                begin(dx + 1)
            for k in (1, 0):
                part = dot_nt(rows_v[dx], w_v[dx, k])
                total[k] = part if dx == 0 else total[k] + part
        theirs[...] = total[1].astype(BF16)
        mine[...] = total[0]

    flat = [p for four in pieces for p in four]
    spec = lambda cols: pl.BlockSpec((rows, cols), lambda i, s: (0, 0))
    return kernel(
        "hidden",
        body,
        [shape_of((rows, hid), F32), shape_of((rows, hid), BF16)],
        (1,),
        [pl.BlockSpec(memory_space=pl.ANY)] * (len(flat) + 2),
        [spec(hid)] * 2,
        block,
        *flat,
        down,
        got,
        scratch=[
            pltpu.VMEM((NX, rows, quarter), BF16),
            pltpu.VMEM((NX, 2, hid, quarter), BF16),
            pltpu.SemaphoreType.DMA((count, NX, NY)),
            pltpu.SemaphoreType.DMA((NX, 2)),
        ],
    )


def pre_grads(block, mine, back, factors):
    rows, hid = mine.shape
    half = rows // NY
    count = len(CHUNKS[0])
    tokens = half // count

    def body(s_ref, m_ref, b_ref, f0, f1, f2, h_ref, t_ref):
        bh = m_ref[...] + b_ref[...].astype(F32)
        h_ref[:, :hid] = (bh * f1[...]).astype(BF16)
        h_ref[:, hid:] = (bh * f2[...]).astype(BF16)
        term = jnp.sum(bh * f0[...], axis=1, keepdims=True)
        flat = jnp.transpose(jnp.broadcast_to(term, (half, 128)))
        for i in range(count):
            t_ref[0, i : i + 1, :] = flat[0:1, i * tokens : (i + 1) * tokens]

    outs = [shape_of((rows, 2 * hid), BF16), shape_of((NY, count, tokens), F32)]
    spec = lambda cols: pl.BlockSpec((half, cols), lambda i, s: (i, 0))
    return kernel(
        "pre_grads",
        body,
        outs,
        (NY,),
        [spec(hid)] * 5,
        [spec(2 * hid), pl.BlockSpec((1, count, tokens), lambda i, s: (i, 0, 0))],
        block,
        mine,
        back,
        *factors,
    )


def input_parts(block, mine, theirs, weights, got):
    rows = mine.shape[0] // NY
    hid = mine.shape[1] // 2
    quarter = weights[0].shape[0] // (NX * NC)
    steps = 2
    wide = quarter // steps
    order = [(dx, h) for dx in (1, 0) for h in range(steps)]

    def body(s_ref, m_ref, t_ref, *refs):
        sources = refs[:4]
        outs = refs[4:8]
        side_v, w_v, o_v, side_sem, sem, out_sem = refs[8:]
        x, c = s_ref[0] // NC, s_ref[0] % NC

        def weight(n, j):
            dx, h = order[n]
            first = pl.multiple_of((2 * (x ^ dx) + c) * quarter + h * wide, wide)
            return pltpu.make_async_copy(sources[j].at[pl.ds(first, wide), :], w_v.at[n, j], sem.at[n, j])

        def side(k):
            return pltpu.make_async_copy((m_ref, t_ref)[k], side_v.at[k], side_sem.at[k])

        def give(which, n, dy):
            cols = pl.ds(order[n][1] * wide, wide)
            return pltpu.make_async_copy(o_v.at[n, dy], outs[which].at[:, cols], out_sem.at[n, dy])

        side(0).start()
        for j in range(4):
            weight(0, j).start()
        side(1).start()
        for j in range(4):
            weight(1, j).start()
        side(0).wait()
        for n, (dx, h) in enumerate(order):
            total = None
            for j in range(4):
                weight(n, j).wait()
                if n == 0 and j == 2:
                    side(1).wait()
                part = dot_nt(side_v[j // 2, :, (j % 2) * hid : (j % 2 + 1) * hid], w_v[n, j])
                total = part if j == 0 else total + part
                if n + 2 < len(order):
                    weight(n + 2, j).start()
            o_v[n, 0] = total[:rows].astype(BF16)
            o_v[n, 1] = total[rows:].astype(BF16)
            give(0 if dx == 1 else 3, n, dx).start()

            @pl.when(c == 1 - dx)
            def _(n=n, dx=dx):
                give(1, n, 1 - dx).start()

            @pl.when(c != 1 - dx)
            def _(n=n, dx=dx):
                give(2, n, 1 - dx).start()

        for n in range(len(order)):
            for dy in range(NY):
                give(0, n, dy).wait()

    far = pl.BlockSpec(memory_space=pl.ANY)
    return kernel(
        "input",
        body,
        [shape_of((rows, quarter), BF16)] * 4,
        (1,),
        [far] * 6,
        [far] * 4,
        block,
        mine,
        theirs,
        *weights,
        *got,
        scratch=[
            pltpu.VMEM((2,) + mine.shape, BF16),
            pltpu.VMEM((len(order), 4, wide, hid), BF16),
            pltpu.VMEM((len(order), NY, rows, wide), BF16),
            pltpu.SemaphoreType.DMA((2,)),
            pltpu.SemaphoreType.DMA((len(order), 4)),
            pltpu.SemaphoreType.DMA((len(order), NY)),
        ],
    )


def add_pieces(block, base, first, second, types):
    rows, cols = base.shape
    part = rows // len(types)
    wide = cols // 2

    def body(s_ref, b_ref, f_ref, g_ref, *outs):
        for i, out in enumerate(outs):
            s = slice(i * part, (i + 1) * part)
            out[...] = (b_ref[s].astype(F32) + f_ref[s].astype(F32) + g_ref[s].astype(F32)).astype(out.dtype)

    spec = lambda n: pl.BlockSpec((n, wide), lambda i, s: (0, i))
    outs = [shape_of((part, cols), t) for t in types]
    return kernel("add", body, outs, (2,), [spec(rows)] * 3, [spec(part)] * len(outs), block, base, first, second)


def add_corner(block, base, corner):
    rows, cols = base.shape

    def body(s_ref, b_ref, c_ref, out):
        out[...] = (b_ref[...].astype(F32) + c_ref[...].astype(F32)).astype(BF16)

    spec = pl.BlockSpec((rows, cols // 2), lambda i, s: (0, i))
    return kernel("corner", body, shape_of(base.shape, BF16), (2,), [spec] * 2, spec, block, base, corner)


def last_sum(block, keep, parts, out_type):
    def body(s_ref, k_ref, *refs):
        total = k_ref[...]
        for ref in refs[:-1]:
            total = total + ref[...].astype(F32)
        refs[-1][...] = total.astype(out_type)

    spec = pl.BlockSpec(keep.shape, lambda i, s: (0, 0))
    return kernel(
        "last", body, shape_of(keep.shape, out_type), (1,), [spec] * (1 + len(parts)), spec, block, keep, *parts
    )


def dense_local(grad_out, gate_weights, slot_lists, saved_gate, saved_up, w_gate, w_up, w_down):
    tokens, quarter = grad_out.shape
    experts = slot_lists.shape[1]
    top_count = gate_weights.shape[1]
    expert = lax.axis_index("expert")
    block = lax.axis_index("tensor")
    z, y = expert // NY, expert % NY
    at_expert, at_block = expert.reshape(1), block.reshape(1)

    down, gate_w, up_w = w_down[0], w_gate[0], w_up[0]
    near, far = CHUNKS
    own, choice_of = pack_rows(grad_out, slot_lists[0], gate_weights.T)

    z2, z1 = send(own, TO_Z[2], "z2"), send(own, TO_Z[1], "z1")
    first0, second0 = send(own, RIGHT, "first0"), send(own, LEFT, "second0")
    got_down = send(down, TO_CORE, "weights")

    z2, z1, first0, second0, got_down, gate_w_, up_w_ = lax.optimization_barrier(
        (z2, z1, first0, second0, got_down, gate_w, up_w)
    )
    first2, second2 = send(z2, RIGHT, "first2"), send(z2, LEFT, "second2")
    third0 = send(first0, LEFT, "third0")
    z3 = send(z2, TO_Z[1], "z3")
    got_gate, got_up = send(gate_w_, TO_CORE, "weights"), send(up_w_, TO_CORE, "weights")

    z1, z3, first2, second2, third0, got_gate, got_up = lax.optimization_barrier(
        (z1, z3, first2, second2, third0, got_gate, got_up)
    )
    third2 = send(first2, LEFT, "third2")
    first1, second1 = send(z1, RIGHT, "first1"), send(z1, LEFT, "second1")
    saved = saved_gate[0], saved_up[0]
    factors_a = prepare(
        at_expert, at_block, [(own, first0, second0), (z2, first2, second2)], *saved, near
    )
    place = after(at_block, factors_a[0])

    weights, got = (gate_w, up_w), (got_gate, got_up)

    def stage_corner(place, chunk, left, corner):
        value = add_corner(place, left, corner)
        return send(value, RIGHT, f"r_left{chunk[0]}"), value

    def stage_add(place, chunk, base, right, left):
        types = [F32 if d == 0 else BF16 for d in chunk]
        totals = add_pieces(place, base, right, left, types)
        return {d: t if d == 0 else send(t, TO_Z[d], f"r_z{d}") for d, t in zip(chunk, totals)}, totals[0]

    mine, theirs = hidden_parts(
        place, [(own, first0, second0, third0), (z2, first2, second2, third2)], down, got_down
    )
    theirs, first1, second1 = lax.optimization_barrier((theirs, first1, second1))
    back = send(theirs, TO_CORE, "swap_bh0")
    first3, second3 = send(z3, RIGHT, "first3"), send(z3, LEFT, "second3")
    third1 = send(first1, LEFT, "third1")
    mine, term_a = pre_grads(after(at_block, mine), mine, back, factors_a)
    theirs = send(mine, TO_CORE, "swap_h0")
    place = at_block
    corner_a, right_a, left_a, base_a = input_parts(place, mine, theirs, weights, got)
    place = after(at_block, base_a)
    corner_a, right_a = send(corner_a, LEFT, "r_corner0"), send(right_a, LEFT, "r_right0")

    first3, _ = lax.optimization_barrier((first3, base_a))
    third3 = send(first3, LEFT, "third3")
    factors_b = prepare(
        at_expert, place, [(z1, first1, second1), (z3, first3, second3)], *saved, far
    )
    place = after(at_block, factors_b[0])
    mine, theirs = hidden_parts(
        place, [(z1, first1, second1, third1), (z3, first3, second3, third3)], down, got_down
    )
    back = send(theirs, TO_CORE, "swap_bh1")
    place = after(at_block, mine)
    left_a, value = stage_corner(place, near, left_a, corner_a)
    place = after(at_block, value)
    mine, term_b = pre_grads(place, mine, back, factors_b)
    theirs = send(mine, TO_CORE, "swap_h1")
    place = at_block
    corner_b, right_b, left_b, base_b = input_parts(place, mine, theirs, weights, got)
    place = after(at_block, base_b)
    corner_b, right_b = send(corner_b, LEFT, "r_corner1"), send(right_b, LEFT, "r_right1")
    sums, value = stage_add(place, near, base_a, right_a, left_a)
    left_b, value = stage_corner(after(at_block, value), far, left_b, corner_b)
    more, _ = stage_add(after(at_block, value, sums[2]), far, base_b, right_b, left_b)
    sums.update(more)
    grad_in = last_sum(at_block, sums[0], [sums[d] for d in (2, 1, 3)], BF16)

    terms = {d: t[:, i] for c, t in ((near, term_a), (far, term_b)) for i, d in enumerate(c)}
    term = jnp.stack([terms[d] for d in range(NZ)], axis=1)
    term = term + send(term, TO_CORE, "t_core")
    term = term + send(after(term, base_b), TO_X, "t_x")
    term = after(term, value)
    term = jnp.stack([term[0], send(term[1], TO_Y, "t_y")], axis=1)
    term = after(term, right_b)
    slots = [term[0]] + [send(term[d], TO_Z[d], f"t_z{d}") for d in range(1, NZ)]
    slot_grad = jnp.zeros((experts, tokens), F32)
    ids = jnp.arange(experts, dtype=jnp.int32)
    for d in range(NZ):
        for dy in range(NY):
            source = (z ^ d) * NY + (y ^ dy)
            slot_grad = jnp.where((ids == source)[:, None], slots[d][dy][None], slot_grad)
    choice_ids = jnp.arange(top_count, dtype=F32)
    chosen = choice_of[:, :, None] == choice_ids[None, None, :]
    grad_gate = jnp.sum(jnp.where(chosen, slot_grad[:, :, None], 0.0), axis=0)
    return (grad_in, grad_gate)


def local(grad_out, gate_weights, slot_lists, *rest):
    tokens = grad_out.shape[0]
    _, experts, capacity = slot_lists.shape
    dense = experts == gate_weights.shape[1] == NZ * NY and capacity == tokens
    dense = dense and lax.axis_size("expert") == NZ * NY and lax.axis_size("tensor") == NX * NC
    program = dense_local if dense else routed_local
    return program(grad_out, gate_weights, slot_lists, *rest)


def solution(mesh):
    in_specs = (
        P("expert", "tensor"),
        P("expert", None),
        P("expert", None, None),
        P("expert", None, "tensor"),
        P("expert", None, "tensor"),
        P("expert", None, "tensor"),
        P("expert", None, "tensor"),
        P("expert", "tensor", None),
    )
    out_specs = (P("expert", "tensor"), P("expert", None))
    return jax.shard_map(local, mesh=mesh, in_specs=in_specs, out_specs=out_specs, check_vma=False)
```

```python
import jax
import jax.numpy as jnp
from jax import lax
from jax.experimental import pallas as pl
from jax.experimental.pallas import tpu as pltpu
from jax.sharding import PartitionSpec as P

BOTH = ("expert", "tensor")
F32 = jnp.float32
BF16 = jnp.bfloat16


def silu_pair(pre_act):
    sigma = jax.nn.sigmoid(pre_act)
    return (pre_act * sigma, sigma * (1.0 + pre_act * (1.0 - sigma)))


def routed_local(grad_out, gate_weights, slot_lists, saved_gate, saved_up, w_gate, w_up, w_down):
    slot_table = slot_lists[0]
    experts, capacity = slot_table.shape
    tok_count, quarter = grad_out.shape
    top_count = gate_weights.shape[1]
    entries = slot_table.reshape(-1)
    occupied = entries >= 0
    owner_token = jnp.where(occupied, entries // top_count, -1)
    picker = owner_token[:, None] == jnp.arange(tok_count, dtype=jnp.int32)[None, :]
    picker_half = picker.astype(jnp.bfloat16)
    send_rows = jnp.dot(picker_half, grad_out, preferred_element_type=jnp.float32).astype(
        jnp.bfloat16
    )
    send_gate = jnp.where(
        occupied, gate_weights.reshape(-1)[jnp.maximum(entries, 0)], jnp.zeros((), jnp.bfloat16)
    )
    got_rows, got_gate = (
        lax.all_to_all(
            send_rows.reshape(experts, capacity, quarter),
            "expert",
            split_axis=0,
            concat_axis=0,
            tiled=True,
        ),
        lax.all_to_all(
            send_gate.reshape(experts, capacity), "expert", split_axis=0, concat_axis=0, tiled=True
        ),
    )
    slot_count = got_rows.shape[0] * capacity
    routed = got_rows.reshape(slot_count, quarter)
    down_proj = w_down[0]
    contract = (((1,), (1,)), ((), ()))
    back_hidden = lax.dot_general(
        lax.all_gather(routed, "tensor", axis=1, tiled=True),
        down_proj,
        contract,
        preferred_element_type=jnp.float32,
    )
    gate_pre = saved_gate[0].astype(jnp.float32)
    up_pre = saved_up[0].astype(jnp.float32)
    activated, derivative = silu_pair(gate_pre)
    hidden = activated * up_pre
    slot_gate_grad = lax.psum(jnp.sum(back_hidden * hidden, axis=1), "tensor")
    scaled = got_gate.reshape(slot_count).astype(jnp.float32)[:, None] * back_hidden
    grad_pre_gate = (scaled * up_pre * derivative).astype(jnp.bfloat16)
    grad_pre_up = (scaled * activated).astype(jnp.bfloat16)
    gate_proj = w_gate[0]
    up_proj = w_up[0]
    partial_rows = lax.dot_general(
        gate_proj, grad_pre_gate, contract, preferred_element_type=jnp.float32
    )
    partial_rows = (
        partial_rows
        + lax.dot_general(up_proj, grad_pre_up, contract, preferred_element_type=jnp.float32)
    ).astype(jnp.bfloat16)
    back_rows = lax.all_to_all(partial_rows, "expert", split_axis=1, concat_axis=1, tiled=True)
    back_gate = lax.all_to_all(
        slot_gate_grad.reshape(1, slot_count), "expert", split_axis=1, concat_axis=1, tiled=True
    )
    local_sums = lax.dot_general(
        picker_half, back_rows, (((0,), (1,)), ((), ())), preferred_element_type=jnp.float32
    )
    grad_in = lax.psum_scatter(
        local_sums.astype(jnp.bfloat16), "tensor", scatter_dimension=1, tiled=True
    )
    position = jnp.where(occupied, entries, tok_count * top_count)
    gate_sums = (
        jnp.zeros((tok_count * top_count + 1,), jnp.float32).at[position].add(back_gate.reshape(-1))
    )
    grad_gate = gate_sums[:-1].reshape(tok_count, top_count)
    return (grad_in, grad_gate)


NZ, NY, NX, NC = 4, 2, 2, 2


def _pairs(move):
    pairs = []
    for z in range(NZ):
        for y in range(NY):
            for x in range(NX):
                for c in range(NC):
                    tz, ty, tx, tc = move(z, y, x, c)
                    pairs.append((((z * NY + y) * NX + x) * NC + c, ((tz * NY + ty) * NX + tx) * NC + tc))
    return pairs


TO_X = _pairs(lambda z, y, x, c: (z, y, 1 - x, c))
TO_Y = _pairs(lambda z, y, x, c: (z, 1 - y, x, c))
TO_CORE = _pairs(lambda z, y, x, c: (z, y, x, 1 - c))
LEFT = _pairs(lambda z, y, x, c: (z, y, 1 - x, c) if c == 0 else (z, 1 - y, x, c))
RIGHT = _pairs(lambda z, y, x, c: (z, 1 - y, x, c) if c == 0 else (z, y, 1 - x, c))
TO_Z = [_pairs(lambda z, y, x, c, d=d: (z ^ d, y, x, c)) for d in range(NZ)]
CHUNKS = ((0, 2), (1, 3))


def send(value, pairs, name="send"):
    with jax.named_scope(name):
        return lax.ppermute(value, BOTH, pairs)


def after(value, *first):
    return lax.optimization_barrier((value, *first))[0]


def dot_nt(a, b):
    return lax.dot_general(a, b, (((1,), (1,)), ((), ())), preferred_element_type=F32)


def shape_of(shape, dtype):
    return jax.ShapeDtypeStruct(shape, dtype)


HINT = pl.CostEstimate(flops=0, transcendentals=0, bytes_accessed=0)
LARGE = pltpu.CompilerParams(vmem_limit_bytes=48 << 20)


def kernel(name, body, outs, grid, in_specs, out_specs, *args, scratch=()):
    return pl.pallas_call(
        body,
        out_shape=outs,
        grid_spec=pltpu.PrefetchScalarGridSpec(
            num_scalar_prefetch=1, grid=grid, in_specs=in_specs, out_specs=out_specs, scratch_shapes=scratch
        ),
        compiler_params=LARGE,
        cost_estimate=HINT,
        name=name,
    )(*args)


META = 8


def pack_rows(grad_out, slots, gates):
    tokens, quarter = grad_out.shape
    experts = slots.shape[0]
    top_count = gates.shape[0]

    def body(g_ref, s_ref, w_ref, out, choice_ref):
        out[:tokens] = g_ref[...]
        entries = s_ref[...]
        owner = lax.div(entries, top_count)
        choice = (entries - owner * top_count).astype(F32)
        owner = owner.astype(F32)
        gate = w_ref[...].astype(F32)
        square = lax.broadcasted_iota(jnp.int32, (tokens, tokens), 0).astype(F32)
        row = lax.broadcasted_iota(jnp.int32, (META, tokens), 0)
        lane = lax.broadcasted_iota(jnp.int32, (META, tokens), 1).astype(F32)
        number = lax.broadcasted_iota(jnp.int32, (top_count, tokens), 0).astype(F32)
        for e in range(experts):
            hit = jnp.where(square == owner[e : e + 1], 1.0, 0.0).astype(BF16)
            value = jnp.where(row == 0, lane, choice[e : e + 1]).astype(BF16)
            found = dot_nt(value, hit)
            chosen = found[1:2]
            weight = jnp.sum(jnp.where(number == chosen, gate, 0.0), axis=0, keepdims=True)
            choice_ref[e : e + 1, :] = chosen
            out[tokens:, e * tokens : (e + 1) * tokens] = jnp.where(row == 0, found, weight).astype(BF16)

    full = lambda shape: pl.BlockSpec(shape, lambda i: (0, 0))
    return pl.pallas_call(
        body,
        out_shape=[shape_of((tokens + META, quarter), BF16), shape_of((experts, tokens), F32)],
        grid=(1,),
        in_specs=[full(grad_out.shape), full(slots.shape), full(gates.shape)],
        out_specs=[full((tokens + META, quarter)), full((experts, tokens))],
        compiler_params=pltpu.CompilerParams(vmem_limit_bytes=60 << 20),
        cost_estimate=HINT,
        name="pack",
    )(grad_out, slots, gates)


def prepare(expert, block, near, saved_gate, saved_up, chunk):
    tokens = near[0][0].shape[0] - META
    hid = saved_gate.shape[1]
    count = len(chunk)
    low, step = chunk[0], chunk[1] - chunk[0]

    def group(i, e, s):
        return ((e[0] // NY) ^ (low + step * (i % count))) * NY + ((e[0] % NY) ^ (i // count))

    def body(e_ref, s_ref, *refs):
        metas = refs[: 3 * count]
        g_ref, u_ref = refs[3 * count : 3 * count + 2]
        outs = refs[3 * count + 2 :]
        i, c = pl.program_id(0), s_ref[0] % NC
        meta = None
        for k in range(count):
            own, first, second = (m[...].astype(F32) for m in metas[3 * k : 3 * k + 3])
            mine = jnp.where(i // count == 0, own, jnp.where(c == 0, first, second))
            meta = mine if meta is None else jnp.where(i % count == k, mine, meta)
        slots = lax.broadcasted_iota(jnp.int32, (tokens, tokens), 0).astype(F32)
        pick = jnp.where(slots == meta[0:1], 1.0, 0.0).astype(BF16)
        flip = (((0,), (0,)), ((), ()))
        gate_pre = lax.dot_general(pick, g_ref[...], flip, preferred_element_type=F32)
        up_pre = lax.dot_general(pick, u_ref[...], flip, preferred_element_type=F32)
        scale = jnp.transpose(jnp.broadcast_to(meta[1:2], (tokens, tokens)))[:, 0:1]
        activated, derivative = silu_pair(gate_pre)
        outs[0][...] = activated * up_pre
        outs[1][...] = scale * up_pre * derivative
        outs[2][...] = scale * activated

    out = shape_of((NY * count * tokens, hid), F32)
    meta = pl.BlockSpec((META, tokens), lambda i, e, s: (tokens // META, e[0]))
    saved = pl.BlockSpec((tokens, hid), lambda i, e, s: (group(i, e, s), 0))
    spec = pl.BlockSpec((tokens, hid), lambda i, e, s: (i, 0))
    flat = [p for three in near for p in three]
    return pl.pallas_call(
        body,
        out_shape=[out] * 3,
        grid_spec=pltpu.PrefetchScalarGridSpec(
            num_scalar_prefetch=2,
            grid=(NY * count,),
            in_specs=[meta] * len(flat) + [saved, saved],
            out_specs=[spec] * 3,
        ),
        compiler_params=LARGE,
        cost_estimate=HINT,
        name="prepare",
    )(expert, block, *flat, saved_gate, saved_up)


def hidden_parts(block, pieces, down, got):
    tokens, quarter = pieces[0][0].shape[0] - META, pieces[0][0].shape[1]
    hid = down.shape[0]
    count = len(pieces)
    half = count * tokens
    rows = NY * half

    def body(s_ref, *refs):
        near = refs[: 4 * count]
        d_ref, o_ref, mine, theirs, rows_v, w_v, row_sem, w_sem = refs[4 * count :]
        x, c = s_ref[0] // NC, s_ref[0] % NC

        def columns(q):
            return pl.ds(pl.multiple_of(q * quarter, quarter), quarter)

        def weight(dx, k):
            source = (d_ref, o_ref)[k].at[:, columns(2 * (x ^ dx) + c)]
            return pltpu.make_async_copy(source, w_v.at[dx, pl.ds(k * hid, hid), :], w_sem.at[dx, k])

        def piece(i, j, dx, dy):
            target = rows_v.at[dx, pl.ds(dy * half + i * tokens, tokens), :]
            source = near[4 * i + j].at[pl.ds(0, tokens), :]
            return pltpu.make_async_copy(source, target, row_sem.at[i, dx, dy])

        def begin(dx):
            for k in (1, 0):
                weight(dx, k).start()
            for i in range(count):
                piece(i, 0 if dx == 0 else 3, dx, dx).start()

                @pl.when(c == dx)
                def _(i=i, dx=dx):
                    piece(i, 1, dx, 1 - dx).start()

                @pl.when(c != dx)
                def _(i=i, dx=dx):
                    piece(i, 2, dx, 1 - dx).start()

        total = None
        begin(0)
        for dx in range(NX):
            for i in range(count):
                for dy in range(NY):
                    piece(i, 0, dx, dy).wait()
            for k in (1, 0):
                weight(dx, k).wait()
            if dx + 1 < NX:
                begin(dx + 1)
            part = dot_nt(rows_v[dx], w_v[dx])
            total = part if dx == 0 else total + part
        mine[...] = total[:, :hid]
        theirs[...] = total[:, hid:].astype(BF16)

    flat = [p for four in pieces for p in four]
    spec = lambda cols: pl.BlockSpec((rows, cols), lambda i, s: (0, 0))
    return kernel(
        "hidden",
        body,
        [shape_of((rows, hid), F32), shape_of((rows, hid), BF16)],
        (1,),
        [pl.BlockSpec(memory_space=pl.ANY)] * (len(flat) + 2),
        [spec(hid)] * 2,
        block,
        *flat,
        down,
        got,
        scratch=[
            pltpu.VMEM((NX, rows, quarter), BF16),
            pltpu.VMEM((NX, 2 * hid, quarter), BF16),
            pltpu.SemaphoreType.DMA((count, NX, NY)),
            pltpu.SemaphoreType.DMA((NX, 2)),
        ],
    )


def pre_grads(block, mine, back, factors):
    rows, hid = mine.shape
    half = rows // NY
    count = len(CHUNKS[0])
    tokens = half // count

    def body(s_ref, m_ref, b_ref, f0, f1, f2, h_ref, t_ref):
        bh = m_ref[...] + b_ref[...].astype(F32)
        h_ref[:, :hid] = (bh * f1[...]).astype(BF16)
        h_ref[:, hid:] = (bh * f2[...]).astype(BF16)
        term = jnp.sum(bh * f0[...], axis=1, keepdims=True)
        flat = jnp.transpose(jnp.broadcast_to(term, (half, 128)))
        for i in range(count):
            t_ref[0, i : i + 1, :] = flat[0:1, i * tokens : (i + 1) * tokens]

    outs = [shape_of((rows, 2 * hid), BF16), shape_of((NY, count, tokens), F32)]
    spec = lambda cols: pl.BlockSpec((half, cols), lambda i, s: (i, 0))
    return kernel(
        "pre_grads",
        body,
        outs,
        (NY,),
        [spec(hid)] * 5,
        [spec(2 * hid), pl.BlockSpec((1, count, tokens), lambda i, s: (i, 0, 0))],
        block,
        mine,
        back,
        *factors,
    )


def input_parts(block, mine, theirs, weights, got):
    rows = mine.shape[0] // NY
    hid = mine.shape[1] // 2
    quarter = weights[0].shape[0] // (NX * NC)
    steps = 2
    wide = quarter // steps
    order = [(dx, h) for dx in (1, 0) for h in range(steps)]

    def body(s_ref, m_ref, t_ref, *refs):
        sources = refs[:4]
        outs = refs[4:8]
        side_v, w_v, o_v, side_sem, sem, out_sem = refs[8:]
        x, c = s_ref[0] // NC, s_ref[0] % NC

        def weight(n, j):
            dx, h = order[n]
            first = pl.multiple_of((2 * (x ^ dx) + c) * quarter + h * wide, wide)
            target = w_v.at[n, j // 2, :, pl.ds((j % 2) * hid, hid)]
            return pltpu.make_async_copy(sources[j].at[pl.ds(first, wide), :], target, sem.at[n, j])

        def side(k):
            return pltpu.make_async_copy((m_ref, t_ref)[k], side_v.at[k], side_sem.at[k])

        def give(which, n, dy):
            cols = pl.ds(order[n][1] * wide, wide)
            return pltpu.make_async_copy(o_v.at[n, dy], outs[which].at[:, cols], out_sem.at[n, dy])

        side(0).start()
        for j in range(4):
            weight(0, j).start()
        side(1).start()
        for j in range(4):
            weight(1, j).start()
        side(0).wait()
        for n, (dx, h) in enumerate(order):
            total = None
            for k in range(2):
                for j in (2 * k, 2 * k + 1):
                    weight(n, j).wait()
                if n == 0 and k == 1:
                    side(1).wait()
                part = dot_nt(side_v[k], w_v[n, k])
                total = part if k == 0 else total + part
                for j in (2 * k, 2 * k + 1):
                    if n + 2 < len(order):
                        weight(n + 2, j).start()
            o_v[n, 0] = total[:rows].astype(BF16)
            o_v[n, 1] = total[rows:].astype(BF16)
            give(0 if dx == 1 else 3, n, dx).start()

            @pl.when(c == 1 - dx)
            def _(n=n, dx=dx):
                give(1, n, 1 - dx).start()

            @pl.when(c != 1 - dx)
            def _(n=n, dx=dx):
                give(2, n, 1 - dx).start()

        for n in range(len(order)):
            for dy in range(NY):
                give(0, n, dy).wait()

    far = pl.BlockSpec(memory_space=pl.ANY)
    return kernel(
        "input",
        body,
        [shape_of((rows, quarter), BF16)] * 4,
        (1,),
        [far] * 6,
        [far] * 4,
        block,
        mine,
        theirs,
        *weights,
        *got,
        scratch=[
            pltpu.VMEM((2,) + mine.shape, BF16),
            pltpu.VMEM((len(order), 2, wide, 2 * hid), BF16),
            pltpu.VMEM((len(order), NY, rows, wide), BF16),
            pltpu.SemaphoreType.DMA((2,)),
            pltpu.SemaphoreType.DMA((len(order), 4)),
            pltpu.SemaphoreType.DMA((len(order), NY)),
        ],
    )


def add_pieces(block, base, first, second, types):
    rows, cols = base.shape
    part = rows // len(types)
    wide = cols // 2

    def body(s_ref, b_ref, f_ref, g_ref, *outs):
        for i, out in enumerate(outs):
            s = slice(i * part, (i + 1) * part)
            out[...] = (b_ref[s].astype(F32) + f_ref[s].astype(F32) + g_ref[s].astype(F32)).astype(out.dtype)

    spec = lambda n: pl.BlockSpec((n, wide), lambda i, s: (0, i))
    outs = [shape_of((part, cols), t) for t in types]
    return kernel("add", body, outs, (2,), [spec(rows)] * 3, [spec(part)] * len(outs), block, base, first, second)


def add_corner(block, base, corner):
    rows, cols = base.shape

    def body(s_ref, b_ref, c_ref, out):
        out[...] = (b_ref[...].astype(F32) + c_ref[...].astype(F32)).astype(BF16)

    spec = pl.BlockSpec((rows, cols // 2), lambda i, s: (0, i))
    return kernel("corner", body, shape_of(base.shape, BF16), (2,), [spec] * 2, spec, block, base, corner)


def last_sum(block, keep, parts, out_type):
    def body(s_ref, k_ref, *refs):
        total = k_ref[...]
        for ref in refs[:-1]:
            total = total + ref[...].astype(F32)
        refs[-1][...] = total.astype(out_type)

    spec = pl.BlockSpec(keep.shape, lambda i, s: (0, 0))
    return kernel(
        "last", body, shape_of(keep.shape, out_type), (1,), [spec] * (1 + len(parts)), spec, block, keep, *parts
    )


def dense_local(grad_out, gate_weights, slot_lists, saved_gate, saved_up, w_gate, w_up, w_down):
    tokens, quarter = grad_out.shape
    experts = slot_lists.shape[1]
    top_count = gate_weights.shape[1]
    expert = lax.axis_index("expert")
    block = lax.axis_index("tensor")
    z, y = expert // NY, expert % NY
    at_expert, at_block = expert.reshape(1), block.reshape(1)

    down, gate_w, up_w = w_down[0], w_gate[0], w_up[0]
    near, far = CHUNKS
    own, choice_of = pack_rows(grad_out, slot_lists[0], gate_weights.T)

    z2, z1 = send(own, TO_Z[2], "z2"), send(own, TO_Z[1], "z1")
    first0, second0 = send(own, RIGHT, "first0"), send(own, LEFT, "second0")
    got_down = send(down, TO_CORE, "weights")

    z2, z1, first0, second0, got_down, gate_w_, up_w_ = lax.optimization_barrier(
        (z2, z1, first0, second0, got_down, gate_w, up_w)
    )
    first2, second2 = send(z2, RIGHT, "first2"), send(z2, LEFT, "second2")
    third0 = send(first0, LEFT, "third0")
    z3 = send(z2, TO_Z[1], "z3")
    got_gate = send(gate_w_, TO_CORE, "weights")

    z1, z3, first2, second2, third0, got_gate, up_w_ = lax.optimization_barrier(
        (z1, z3, first2, second2, third0, got_gate, up_w_)
    )
    got_up = send(up_w_, TO_CORE, "weights")
    third2 = send(first2, LEFT, "third2")
    first1, second1 = send(z1, RIGHT, "first1"), send(z1, LEFT, "second1")
    first3 = send(z3, RIGHT, "first3")
    saved = saved_gate[0], saved_up[0]
    factors_a = prepare(
        at_expert, at_block, [(own, first0, second0), (z2, first2, second2)], *saved, near
    )
    place = after(at_block, factors_a[0])

    weights, got = (gate_w, up_w), (got_gate, got_up)

    def stage_corner(place, chunk, left, corner):
        value = add_corner(place, left, corner)
        return send(value, RIGHT, f"r_left{chunk[0]}"), value

    def stage_add(place, chunk, base, right, left):
        types = [F32 if d == 0 else BF16 for d in chunk]
        totals = add_pieces(place, base, right, left, types)
        return {d: t if d == 0 else send(t, TO_Z[d], f"r_z{d}") for d, t in zip(chunk, totals)}, totals[0]

    mine, theirs = hidden_parts(
        place, [(own, first0, second0, third0), (z2, first2, second2, third2)], down, got_down
    )
    theirs, first1, second1, got_up, first3 = lax.optimization_barrier((theirs, first1, second1, got_up, first3))
    back = send(theirs, TO_CORE, "swap_bh0")
    second3 = send(z3, LEFT, "second3")
    third3 = send(first3, LEFT, "third3")
    third1 = send(first1, LEFT, "third1")
    mine, term_a = pre_grads(after(at_block, mine), mine, back, factors_a)
    theirs = send(mine, TO_CORE, "swap_h0")
    place = at_block
    corner_a, right_a, left_a, base_a = input_parts(place, mine, theirs, weights, got)
    place = after(at_block, base_a)
    corner_a, right_a = send(corner_a, LEFT, "r_corner0"), send(right_a, LEFT, "r_right0")

    factors_b = prepare(
        at_expert, place, [(z1, first1, second1), (z3, first3, second3)], *saved, far
    )
    place = after(at_block, factors_b[0])
    mine, theirs = hidden_parts(
        place, [(z1, first1, second1, third1), (z3, first3, second3, third3)], down, got_down
    )
    back = send(theirs, TO_CORE, "swap_bh1")
    place = after(at_block, mine)
    left_a, value = stage_corner(place, near, left_a, corner_a)
    place = after(at_block, value)
    mine, term_b = pre_grads(place, mine, back, factors_b)
    theirs = send(mine, TO_CORE, "swap_h1")
    place = at_block
    corner_b, right_b, left_b, base_b = input_parts(place, mine, theirs, weights, got)
    place = after(at_block, base_b)
    corner_b, right_b = send(corner_b, LEFT, "r_corner1"), send(right_b, LEFT, "r_right1")
    sums, value = stage_add(place, near, base_a, right_a, left_a)
    left_b, value = stage_corner(after(at_block, value), far, left_b, corner_b)
    more, kept = stage_add(after(at_block, value, sums[2]), far, base_b, right_b, left_b)
    sums.update(more)
    grad_in = last_sum(at_block, sums[0], [sums[d] for d in (2, 1, 3)], BF16)

    terms = {d: t[:, i] for c, t in ((near, term_a), (far, term_b)) for i, d in enumerate(c)}
    term = jnp.stack([terms[d] for d in range(NZ)], axis=1)
    term = term + send(term, TO_CORE, "t_core")
    term = term + send(after(term, base_b), TO_X, "t_x")
    term = after(term, value)
    term = jnp.stack([term[0], send(term[1], TO_Y, "t_y")], axis=1)
    term = after(term, kept)
    slots = [term[0]] + [send(term[d], TO_Z[d], f"t_z{d}") for d in range(1, NZ)]
    slot_grad = jnp.zeros((experts, tokens), F32)
    ids = jnp.arange(experts, dtype=jnp.int32)
    for d in range(NZ):
        for dy in range(NY):
            source = (z ^ d) * NY + (y ^ dy)
            slot_grad = jnp.where((ids == source)[:, None], slots[d][dy][None], slot_grad)
    choice_ids = jnp.arange(top_count, dtype=F32)
    chosen = choice_of[:, :, None] == choice_ids[None, None, :]
    grad_gate = jnp.sum(jnp.where(chosen, slot_grad[:, :, None], 0.0), axis=0)
    return (grad_in, grad_gate)


def local(grad_out, gate_weights, slot_lists, *rest):
    tokens = grad_out.shape[0]
    _, experts, capacity = slot_lists.shape
    dense = experts == gate_weights.shape[1] == NZ * NY and capacity == tokens
    dense = dense and lax.axis_size("expert") == NZ * NY and lax.axis_size("tensor") == NX * NC
    program = dense_local if dense else routed_local
    return program(grad_out, gate_weights, slot_lists, *rest)


def solution(mesh):
    in_specs = (
        P("expert", "tensor"),
        P("expert", None),
        P("expert", None, None),
        P("expert", None, "tensor"),
        P("expert", None, "tensor"),
        P("expert", None, "tensor"),
        P("expert", None, "tensor"),
        P("expert", "tensor", None),
    )
    out_specs = (P("expert", "tensor"), P("expert", None))
    return jax.shard_map(local, mesh=mesh, in_specs=in_specs, out_specs=out_specs, check_vma=False)
```

```python
import jax
import jax.numpy as jnp
from jax import lax
from jax.experimental import pallas as pl
from jax.experimental.pallas import tpu as pltpu
from jax.sharding import PartitionSpec as P

BOTH = ("expert", "tensor")
F32 = jnp.float32
BF16 = jnp.bfloat16


def silu_pair(pre_act):
    sigma = jax.nn.sigmoid(pre_act)
    return (pre_act * sigma, sigma * (1.0 + pre_act * (1.0 - sigma)))


def routed_local(grad_out, gate_weights, slot_lists, saved_gate, saved_up, w_gate, w_up, w_down):
    slot_table = slot_lists[0]
    experts, capacity = slot_table.shape
    tok_count, quarter = grad_out.shape
    top_count = gate_weights.shape[1]
    entries = slot_table.reshape(-1)
    occupied = entries >= 0
    owner_token = jnp.where(occupied, entries // top_count, -1)
    picker = owner_token[:, None] == jnp.arange(tok_count, dtype=jnp.int32)[None, :]
    picker_half = picker.astype(jnp.bfloat16)
    send_rows = jnp.dot(picker_half, grad_out, preferred_element_type=jnp.float32).astype(
        jnp.bfloat16
    )
    send_gate = jnp.where(
        occupied, gate_weights.reshape(-1)[jnp.maximum(entries, 0)], jnp.zeros((), jnp.bfloat16)
    )
    got_rows, got_gate = (
        lax.all_to_all(
            send_rows.reshape(experts, capacity, quarter),
            "expert",
            split_axis=0,
            concat_axis=0,
            tiled=True,
        ),
        lax.all_to_all(
            send_gate.reshape(experts, capacity), "expert", split_axis=0, concat_axis=0, tiled=True
        ),
    )
    slot_count = got_rows.shape[0] * capacity
    routed = got_rows.reshape(slot_count, quarter)
    down_proj = w_down[0]
    contract = (((1,), (1,)), ((), ()))
    back_hidden = lax.dot_general(
        lax.all_gather(routed, "tensor", axis=1, tiled=True),
        down_proj,
        contract,
        preferred_element_type=jnp.float32,
    )
    gate_pre = saved_gate[0].astype(jnp.float32)
    up_pre = saved_up[0].astype(jnp.float32)
    activated, derivative = silu_pair(gate_pre)
    hidden = activated * up_pre
    slot_gate_grad = lax.psum(jnp.sum(back_hidden * hidden, axis=1), "tensor")
    scaled = got_gate.reshape(slot_count).astype(jnp.float32)[:, None] * back_hidden
    grad_pre_gate = (scaled * up_pre * derivative).astype(jnp.bfloat16)
    grad_pre_up = (scaled * activated).astype(jnp.bfloat16)
    gate_proj = w_gate[0]
    up_proj = w_up[0]
    partial_rows = lax.dot_general(
        gate_proj, grad_pre_gate, contract, preferred_element_type=jnp.float32
    )
    partial_rows = (
        partial_rows
        + lax.dot_general(up_proj, grad_pre_up, contract, preferred_element_type=jnp.float32)
    ).astype(jnp.bfloat16)
    back_rows = lax.all_to_all(partial_rows, "expert", split_axis=1, concat_axis=1, tiled=True)
    back_gate = lax.all_to_all(
        slot_gate_grad.reshape(1, slot_count), "expert", split_axis=1, concat_axis=1, tiled=True
    )
    local_sums = lax.dot_general(
        picker_half, back_rows, (((0,), (1,)), ((), ())), preferred_element_type=jnp.float32
    )
    grad_in = lax.psum_scatter(
        local_sums.astype(jnp.bfloat16), "tensor", scatter_dimension=1, tiled=True
    )
    position = jnp.where(occupied, entries, tok_count * top_count)
    gate_sums = (
        jnp.zeros((tok_count * top_count + 1,), jnp.float32).at[position].add(back_gate.reshape(-1))
    )
    grad_gate = gate_sums[:-1].reshape(tok_count, top_count)
    return (grad_in, grad_gate)


NZ, NY, NX, NC = 4, 2, 2, 2


def _pairs(move):
    pairs = []
    for z in range(NZ):
        for y in range(NY):
            for x in range(NX):
                for c in range(NC):
                    tz, ty, tx, tc = move(z, y, x, c)
                    pairs.append((((z * NY + y) * NX + x) * NC + c, ((tz * NY + ty) * NX + tx) * NC + tc))
    return pairs


TO_X = _pairs(lambda z, y, x, c: (z, y, 1 - x, c))
TO_Y = _pairs(lambda z, y, x, c: (z, 1 - y, x, c))
TO_CORE = _pairs(lambda z, y, x, c: (z, y, x, 1 - c))
LEFT = _pairs(lambda z, y, x, c: (z, y, 1 - x, c) if c == 0 else (z, 1 - y, x, c))
RIGHT = _pairs(lambda z, y, x, c: (z, 1 - y, x, c) if c == 0 else (z, y, 1 - x, c))
TO_Z = [_pairs(lambda z, y, x, c, d=d: (z ^ d, y, x, c)) for d in range(NZ)]
CHUNKS = ((0, 2), (1, 3))


def send(value, pairs, name="send"):
    with jax.named_scope(name):
        return lax.ppermute(value, BOTH, pairs)


def after(value, *first):
    return lax.optimization_barrier((value, *first))[0]


def dot_nt(a, b):
    return lax.dot_general(a, b, (((1,), (1,)), ((), ())), preferred_element_type=F32)


def shape_of(shape, dtype):
    return jax.ShapeDtypeStruct(shape, dtype)


HINT = pl.CostEstimate(flops=0, transcendentals=0, bytes_accessed=0)
LARGE = pltpu.CompilerParams(vmem_limit_bytes=48 << 20)


def kernel(name, body, outs, grid, in_specs, out_specs, *args, scratch=()):
    return pl.pallas_call(
        body,
        out_shape=outs,
        grid_spec=pltpu.PrefetchScalarGridSpec(
            num_scalar_prefetch=1, grid=grid, in_specs=in_specs, out_specs=out_specs, scratch_shapes=scratch
        ),
        compiler_params=LARGE,
        cost_estimate=HINT,
        name=name,
    )(*args)


META = 8


def pack_rows(grad_out, slots, gates):
    tokens, quarter = grad_out.shape
    experts = slots.shape[0]
    top_count = gates.shape[0]

    def body(g_ref, s_ref, w_ref, out, choice_ref):
        out[:tokens] = g_ref[...]
        entries = s_ref[...]
        owner = lax.div(entries, top_count)
        choice = (entries - owner * top_count).astype(F32)
        owner = owner.astype(F32)
        gate = w_ref[...].astype(F32)
        square = lax.broadcasted_iota(jnp.int32, (tokens, tokens), 0).astype(F32)
        row = lax.broadcasted_iota(jnp.int32, (META, tokens), 0)
        lane = lax.broadcasted_iota(jnp.int32, (META, tokens), 1).astype(F32)
        number = lax.broadcasted_iota(jnp.int32, (top_count, tokens), 0).astype(F32)
        for e in range(experts):
            hit = jnp.where(square == owner[e : e + 1], 1.0, 0.0).astype(BF16)
            value = jnp.where(row == 0, lane, choice[e : e + 1]).astype(BF16)
            found = dot_nt(value, hit)
            chosen = found[1:2]
            weight = jnp.sum(jnp.where(number == chosen, gate, 0.0), axis=0, keepdims=True)
            choice_ref[e : e + 1, :] = chosen
            out[tokens:, e * tokens : (e + 1) * tokens] = jnp.where(row == 0, found, weight).astype(BF16)

    full = lambda shape: pl.BlockSpec(shape, lambda i: (0, 0))
    return pl.pallas_call(
        body,
        out_shape=[shape_of((tokens + META, quarter), BF16), shape_of((experts, tokens), F32)],
        grid=(1,),
        in_specs=[full(grad_out.shape), full(slots.shape), full(gates.shape)],
        out_specs=[full((tokens + META, quarter)), full((experts, tokens))],
        compiler_params=pltpu.CompilerParams(vmem_limit_bytes=60 << 20),
        cost_estimate=HINT,
        name="pack",
    )(grad_out, slots, gates)


def prepare(expert, block, near, saved_gate, saved_up, chunk):
    tokens = near[0][0].shape[0] - META
    hid = saved_gate.shape[1]
    count = len(chunk)
    low, step = chunk[0], chunk[1] - chunk[0]

    def group(i, e, s):
        return ((e[0] // NY) ^ (low + step * (i % count))) * NY + ((e[0] % NY) ^ (i // count))

    def body(e_ref, s_ref, *refs):
        metas = refs[: 3 * count]
        g_ref, u_ref = refs[3 * count : 3 * count + 2]
        outs = refs[3 * count + 2 :]
        i, c = pl.program_id(0), s_ref[0] % NC
        meta = None
        for k in range(count):
            own, first, second = (m[...].astype(F32) for m in metas[3 * k : 3 * k + 3])
            mine = jnp.where(i // count == 0, own, jnp.where(c == 0, first, second))
            meta = mine if meta is None else jnp.where(i % count == k, mine, meta)
        slots = lax.broadcasted_iota(jnp.int32, (tokens, tokens), 0).astype(F32)
        pick = jnp.where(slots == meta[0:1], 1.0, 0.0).astype(BF16)
        flip = (((0,), (0,)), ((), ()))
        gate_pre = lax.dot_general(pick, g_ref[...], flip, preferred_element_type=F32)
        up_pre = lax.dot_general(pick, u_ref[...], flip, preferred_element_type=F32)
        scale = jnp.transpose(jnp.broadcast_to(meta[1:2], (tokens, tokens)))[:, 0:1]
        activated, derivative = silu_pair(gate_pre)
        outs[0][...] = activated * up_pre
        outs[1][...] = scale * up_pre * derivative
        outs[2][...] = scale * activated

    out = shape_of((NY * count * tokens, hid), F32)
    meta = pl.BlockSpec((META, tokens), lambda i, e, s: (tokens // META, e[0]))
    saved = pl.BlockSpec((tokens, hid), lambda i, e, s: (group(i, e, s), 0))
    spec = pl.BlockSpec((tokens, hid), lambda i, e, s: (i, 0))
    flat = [p for three in near for p in three]
    return pl.pallas_call(
        body,
        out_shape=[out] * 3,
        grid_spec=pltpu.PrefetchScalarGridSpec(
            num_scalar_prefetch=2,
            grid=(NY * count,),
            in_specs=[meta] * len(flat) + [saved, saved],
            out_specs=[spec] * 3,
        ),
        compiler_params=LARGE,
        cost_estimate=HINT,
        name="prepare",
    )(expert, block, *flat, saved_gate, saved_up)


def hidden_parts(block, pieces, down, got):
    tokens, quarter = pieces[0][0].shape[0] - META, pieces[0][0].shape[1]
    hid = down.shape[0]
    count = len(pieces)
    half = count * tokens
    rows = NY * half

    def body(s_ref, *refs):
        near = refs[: 4 * count]
        d_ref, o_ref, mine, theirs, rows_v, w_v, row_sem, w_sem = refs[4 * count :]
        x, c = s_ref[0] // NC, s_ref[0] % NC

        def columns(q):
            return pl.ds(pl.multiple_of(q * quarter, quarter), quarter)

        def weight(dx, k):
            source = (d_ref, o_ref)[k].at[:, columns(2 * (x ^ dx) + c)]
            return pltpu.make_async_copy(source, w_v.at[dx, pl.ds(k * hid, hid), :], w_sem.at[dx, k])

        def piece(i, j, dx, dy):
            target = rows_v.at[dx, pl.ds(dy * half + i * tokens, tokens), :]
            source = near[4 * i + j].at[pl.ds(0, tokens), :]
            return pltpu.make_async_copy(source, target, row_sem.at[i, dx, dy])

        def begin(dx):
            for k in (1, 0):
                weight(dx, k).start()
            for i in range(count):
                piece(i, 0 if dx == 0 else 3, dx, dx).start()

                @pl.when(c == dx)
                def _(i=i, dx=dx):
                    piece(i, 1, dx, 1 - dx).start()

                @pl.when(c != dx)
                def _(i=i, dx=dx):
                    piece(i, 2, dx, 1 - dx).start()

        total = None
        begin(0)
        for dx in range(NX):
            for i in range(count):
                for dy in range(NY):
                    piece(i, 0, dx, dy).wait()
            for k in (1, 0):
                weight(dx, k).wait()
            if dx + 1 < NX:
                begin(dx + 1)
            part = dot_nt(rows_v[dx], w_v[dx])
            total = part if dx == 0 else total + part
        mine[...] = total[:, :hid]
        theirs[...] = total[:, hid:].astype(BF16)

    flat = [p for four in pieces for p in four]
    spec = lambda cols: pl.BlockSpec((rows, cols), lambda i, s: (0, 0))
    return kernel(
        "hidden",
        body,
        [shape_of((rows, hid), F32), shape_of((rows, hid), BF16)],
        (1,),
        [pl.BlockSpec(memory_space=pl.ANY)] * (len(flat) + 2),
        [spec(hid)] * 2,
        block,
        *flat,
        down,
        got,
        scratch=[
            pltpu.VMEM((NX, rows, quarter), BF16),
            pltpu.VMEM((NX, 2 * hid, quarter), BF16),
            pltpu.SemaphoreType.DMA((count, NX, NY)),
            pltpu.SemaphoreType.DMA((NX, 2)),
        ],
    )


def pre_grads(block, mine, back, factors):
    rows, hid = mine.shape
    half = rows // NY
    count = len(CHUNKS[0])
    tokens = half // count

    def body(s_ref, m_ref, b_ref, f0, f1, f2, h_ref, t_ref):
        bh = m_ref[...] + b_ref[...].astype(F32)
        h_ref[:, :hid] = (bh * f1[...]).astype(BF16)
        h_ref[:, hid:] = (bh * f2[...]).astype(BF16)
        term = jnp.sum(bh * f0[...], axis=1, keepdims=True)
        flat = jnp.transpose(jnp.broadcast_to(term, (half, 128)))
        for i in range(count):
            t_ref[0, i : i + 1, :] = flat[0:1, i * tokens : (i + 1) * tokens]

    outs = [shape_of((rows, 2 * hid), BF16), shape_of((NY, count, tokens), F32)]
    spec = lambda cols: pl.BlockSpec((half, cols), lambda i, s: (i, 0))
    return kernel(
        "pre_grads",
        body,
        outs,
        (NY,),
        [spec(hid)] * 5,
        [spec(2 * hid), pl.BlockSpec((1, count, tokens), lambda i, s: (i, 0, 0))],
        block,
        mine,
        back,
        *factors,
    )


def input_parts(block, mine, theirs, weights, got):
    rows = mine.shape[0] // NY
    hid = mine.shape[1] // 2
    quarter = weights[0].shape[0] // (NX * NC)
    steps = 2
    wide = quarter // steps
    order = [(dx, h) for dx in (1, 0) for h in range(steps)]

    def body(s_ref, m_ref, t_ref, *refs):
        sources = refs[:4]
        outs = refs[4:8]
        side_v, w_v, o_v, side_sem, sem, out_sem = refs[8:]
        x, c = s_ref[0] // NC, s_ref[0] % NC

        def weight(n, j):
            dx, h = order[n]
            first = pl.multiple_of((2 * (x ^ dx) + c) * quarter + h * wide, wide)
            target = w_v.at[n, j // 2, :, pl.ds((j % 2) * hid, hid)]
            return pltpu.make_async_copy(sources[j].at[pl.ds(first, wide), :], target, sem.at[n, j])

        def side(k):
            return pltpu.make_async_copy((m_ref, t_ref)[k], side_v.at[k], side_sem.at[k])

        def give(which, n, dy):
            cols = pl.ds(order[n][1] * wide, wide)
            return pltpu.make_async_copy(o_v.at[n, dy], outs[which].at[:, cols], out_sem.at[n, dy])

        side(0).start()
        for j in range(4):
            weight(0, j).start()
        side(1).start()
        for j in range(4):
            weight(1, j).start()
        side(0).wait()
        for n, (dx, h) in enumerate(order):
            total = None
            for k in range(2):
                for j in (2 * k, 2 * k + 1):
                    weight(n, j).wait()
                if n == 0 and k == 1:
                    side(1).wait()
                part = dot_nt(side_v[k], w_v[n, k])
                total = part if k == 0 else total + part
                for j in (2 * k, 2 * k + 1):
                    if n + 2 < len(order):
                        weight(n + 2, j).start()
            o_v[n, 0] = total[:rows].astype(BF16)
            o_v[n, 1] = total[rows:].astype(BF16)
            give(0 if dx == 1 else 3, n, dx).start()

            @pl.when(c == 1 - dx)
            def _(n=n, dx=dx):
                give(1, n, 1 - dx).start()

            @pl.when(c != 1 - dx)
            def _(n=n, dx=dx):
                give(2, n, 1 - dx).start()

        for n in range(len(order)):
            for dy in range(NY):
                give(0, n, dy).wait()

    far = pl.BlockSpec(memory_space=pl.ANY)
    return kernel(
        "input",
        body,
        [shape_of((rows, quarter), BF16)] * 4,
        (1,),
        [far] * 6,
        [far] * 4,
        block,
        mine,
        theirs,
        *weights,
        *got,
        scratch=[
            pltpu.VMEM((2,) + mine.shape, BF16),
            pltpu.VMEM((len(order), 2, wide, 2 * hid), BF16),
            pltpu.VMEM((len(order), NY, rows, wide), BF16),
            pltpu.SemaphoreType.DMA((2,)),
            pltpu.SemaphoreType.DMA((len(order), 4)),
            pltpu.SemaphoreType.DMA((len(order), NY)),
        ],
    )


def add_pieces(block, base, first, second, types):
    rows, cols = base.shape
    part = rows // len(types)
    wide = cols // 2

    def body(s_ref, b_ref, f_ref, g_ref, *outs):
        for i, out in enumerate(outs):
            s = slice(i * part, (i + 1) * part)
            out[...] = (b_ref[s].astype(F32) + f_ref[s].astype(F32) + g_ref[s].astype(F32)).astype(out.dtype)

    spec = lambda n: pl.BlockSpec((n, wide), lambda i, s: (0, i))
    outs = [shape_of((part, cols), t) for t in types]
    return kernel("add", body, outs, (2,), [spec(rows)] * 3, [spec(part)] * len(outs), block, base, first, second)


def add_corner(block, base, corner):
    rows, cols = base.shape

    def body(s_ref, b_ref, c_ref, out):
        out[...] = (b_ref[...].astype(F32) + c_ref[...].astype(F32)).astype(BF16)

    spec = pl.BlockSpec((rows, cols // 2), lambda i, s: (0, i))
    return kernel("corner", body, shape_of(base.shape, BF16), (2,), [spec] * 2, spec, block, base, corner)


def last_sum(block, keep, parts, out_type):
    def body(s_ref, k_ref, *refs):
        total = k_ref[...]
        for ref in refs[:-1]:
            total = total + ref[...].astype(F32)
        refs[-1][...] = total.astype(out_type)

    spec = pl.BlockSpec(keep.shape, lambda i, s: (0, 0))
    return kernel(
        "last", body, shape_of(keep.shape, out_type), (1,), [spec] * (1 + len(parts)), spec, block, keep, *parts
    )


def dense_local(grad_out, gate_weights, slot_lists, saved_gate, saved_up, w_gate, w_up, w_down):
    tokens, quarter = grad_out.shape
    experts = slot_lists.shape[1]
    top_count = gate_weights.shape[1]
    expert = lax.axis_index("expert")
    block = lax.axis_index("tensor")
    z, y = expert // NY, expert % NY
    at_expert, at_block = expert.reshape(1), block.reshape(1)

    down, gate_w, up_w = w_down[0], w_gate[0], w_up[0]
    near, far = CHUNKS
    own, choice_of = pack_rows(grad_out, slot_lists[0], gate_weights.T)

    z2, z1 = send(own, TO_Z[2], "z2"), send(own, TO_Z[1], "z1")
    first0, second0 = send(own, RIGHT, "first0"), send(own, LEFT, "second0")
    got_down = send(down, TO_CORE, "weights")

    z2, z1, first0, second0, got_down, gate_w_, up_w_ = lax.optimization_barrier(
        (z2, z1, first0, second0, got_down, gate_w, up_w)
    )
    first2, second2 = send(z2, RIGHT, "first2"), send(z2, LEFT, "second2")
    third0 = send(first0, LEFT, "third0")
    z3 = send(z2, TO_Z[1], "z3")
    got_gate = send(gate_w_, TO_CORE, "weights")

    z1, z3, first2, second2, third0, got_gate, up_w_ = lax.optimization_barrier(
        (z1, z3, first2, second2, third0, got_gate, up_w_)
    )
    got_up = send(up_w_, TO_CORE, "weights")
    third2 = send(first2, LEFT, "third2")
    first1, second1 = send(z1, RIGHT, "first1"), send(z1, LEFT, "second1")
    first3 = send(z3, RIGHT, "first3")
    saved = saved_gate[0], saved_up[0]
    factors_a = prepare(
        at_expert, at_block, [(own, first0, second0), (z2, first2, second2)], *saved, near
    )
    place = after(at_block, factors_a[0])

    weights, got = (gate_w, up_w), (got_gate, got_up)

    def stage_corner(place, chunk, left, corner):
        value = add_corner(place, left, corner)
        return send(value, RIGHT, f"r_left{chunk[0]}"), value

    def stage_add(place, chunk, base, right, left):
        types = [F32 if d == 0 else BF16 for d in chunk]
        totals = add_pieces(place, base, right, left, types)
        return {d: t if d == 0 else send(t, TO_Z[d], f"r_z{d}") for d, t in zip(chunk, totals)}, totals[0]

    mine, theirs = hidden_parts(
        place, [(own, first0, second0, third0), (z2, first2, second2, third2)], down, got_down
    )
    theirs, first1, second1, got_up, first3 = lax.optimization_barrier((theirs, first1, second1, got_up, first3))
    back = send(theirs, TO_CORE, "swap_bh0")
    second3 = send(z3, LEFT, "second3")
    third3 = send(first3, LEFT, "third3")
    third1 = send(first1, LEFT, "third1")
    mine, term_a = pre_grads(after(at_block, mine), mine, back, factors_a)
    theirs = send(mine, TO_CORE, "swap_h0")
    place = at_block
    corner_a, right_a, left_a, base_a = input_parts(place, mine, theirs, weights, got)
    place = after(at_block, base_a)
    corner_a, right_a = send(corner_a, LEFT, "r_corner0"), send(right_a, LEFT, "r_right0")

    factors_b = prepare(
        at_expert, place, [(z1, first1, second1), (z3, first3, second3)], *saved, far
    )
    place = after(at_block, factors_b[0])
    mine, theirs = hidden_parts(
        place, [(z1, first1, second1, third1), (z3, first3, second3, third3)], down, got_down
    )
    back = send(theirs, TO_CORE, "swap_bh1")
    place = after(at_block, mine)
    left_a, value = stage_corner(place, near, left_a, corner_a)
    place = after(at_block, value)
    mine, term_b = pre_grads(place, mine, back, factors_b)
    theirs = send(mine, TO_CORE, "swap_h1")
    place = at_block
    corner_b, right_b, left_b, base_b = input_parts(place, mine, theirs, weights, got)
    place = after(at_block, base_b)
    corner_b, right_b = send(corner_b, LEFT, "r_corner1"), send(right_b, LEFT, "r_right1")
    sums, value = stage_add(place, near, base_a, right_a, left_a)
    left_b, value = stage_corner(after(at_block, value), far, left_b, corner_b)
    early = sums[2]
    more, kept = stage_add(after(at_block, value), far, base_b, right_b, left_b)
    sums.update(more)
    grad_in = last_sum(at_block, sums[0], [sums[d] for d in (2, 1, 3)], BF16)

    terms = {d: t[:, i] for c, t in ((near, term_a), (far, term_b)) for i, d in enumerate(c)}
    term = jnp.stack([terms[d] for d in range(NZ)], axis=1)
    term = term + send(term, TO_CORE, "t_core")
    term = term + send(after(term, base_b), TO_X, "t_x")
    term = after(term, value)
    term = jnp.stack([term[0], send(term[1], TO_Y, "t_y")], axis=1)
    term = after(term, kept, early)
    slots = [term[0]] + [send(term[d], TO_Z[d], f"t_z{d}") for d in range(1, NZ)]
    slot_grad = jnp.zeros((experts, tokens), F32)
    ids = jnp.arange(experts, dtype=jnp.int32)
    for d in range(NZ):
        for dy in range(NY):
            source = (z ^ d) * NY + (y ^ dy)
            slot_grad = jnp.where((ids == source)[:, None], slots[d][dy][None], slot_grad)
    choice_ids = jnp.arange(top_count, dtype=F32)
    chosen = choice_of[:, :, None] == choice_ids[None, None, :]
    grad_gate = jnp.sum(jnp.where(chosen, slot_grad[:, :, None], 0.0), axis=0)
    return (grad_in, grad_gate)


def local(grad_out, gate_weights, slot_lists, *rest):
    tokens = grad_out.shape[0]
    _, experts, capacity = slot_lists.shape
    dense = experts == gate_weights.shape[1] == NZ * NY and capacity == tokens
    dense = dense and lax.axis_size("expert") == NZ * NY and lax.axis_size("tensor") == NX * NC
    program = dense_local if dense else routed_local
    return program(grad_out, gate_weights, slot_lists, *rest)


def solution(mesh):
    in_specs = (
        P("expert", "tensor"),
        P("expert", None),
        P("expert", None, None),
        P("expert", None, "tensor"),
        P("expert", None, "tensor"),
        P("expert", None, "tensor"),
        P("expert", None, "tensor"),
        P("expert", "tensor", None),
    )
    out_specs = (P("expert", "tensor"), P("expert", None))
    return jax.shard_map(local, mesh=mesh, in_specs=in_specs, out_specs=out_specs, check_vma=False)
```

```python
import jax
import jax.numpy as jnp
from jax import lax
from jax.experimental import pallas as pl
from jax.experimental.pallas import tpu as pltpu
from jax.sharding import PartitionSpec as P

BOTH = ("expert", "tensor")
F32 = jnp.float32
BF16 = jnp.bfloat16


def silu_pair(pre_act):
    sigma = jax.nn.sigmoid(pre_act)
    return (pre_act * sigma, sigma * (1.0 + pre_act * (1.0 - sigma)))


def routed_local(grad_out, gate_weights, slot_lists, saved_gate, saved_up, w_gate, w_up, w_down):
    slot_table = slot_lists[0]
    experts, capacity = slot_table.shape
    tok_count, quarter = grad_out.shape
    top_count = gate_weights.shape[1]
    entries = slot_table.reshape(-1)
    occupied = entries >= 0
    owner_token = jnp.where(occupied, entries // top_count, -1)
    picker = owner_token[:, None] == jnp.arange(tok_count, dtype=jnp.int32)[None, :]
    picker_half = picker.astype(jnp.bfloat16)
    send_rows = jnp.dot(picker_half, grad_out, preferred_element_type=jnp.float32).astype(
        jnp.bfloat16
    )
    send_gate = jnp.where(
        occupied, gate_weights.reshape(-1)[jnp.maximum(entries, 0)], jnp.zeros((), jnp.bfloat16)
    )
    got_rows, got_gate = (
        lax.all_to_all(
            send_rows.reshape(experts, capacity, quarter),
            "expert",
            split_axis=0,
            concat_axis=0,
            tiled=True,
        ),
        lax.all_to_all(
            send_gate.reshape(experts, capacity), "expert", split_axis=0, concat_axis=0, tiled=True
        ),
    )
    slot_count = got_rows.shape[0] * capacity
    routed = got_rows.reshape(slot_count, quarter)
    down_proj = w_down[0]
    contract = (((1,), (1,)), ((), ()))
    back_hidden = lax.dot_general(
        lax.all_gather(routed, "tensor", axis=1, tiled=True),
        down_proj,
        contract,
        preferred_element_type=jnp.float32,
    )
    gate_pre = saved_gate[0].astype(jnp.float32)
    up_pre = saved_up[0].astype(jnp.float32)
    activated, derivative = silu_pair(gate_pre)
    hidden = activated * up_pre
    slot_gate_grad = lax.psum(jnp.sum(back_hidden * hidden, axis=1), "tensor")
    scaled = got_gate.reshape(slot_count).astype(jnp.float32)[:, None] * back_hidden
    grad_pre_gate = (scaled * up_pre * derivative).astype(jnp.bfloat16)
    grad_pre_up = (scaled * activated).astype(jnp.bfloat16)
    gate_proj = w_gate[0]
    up_proj = w_up[0]
    partial_rows = lax.dot_general(
        gate_proj, grad_pre_gate, contract, preferred_element_type=jnp.float32
    )
    partial_rows = (
        partial_rows
        + lax.dot_general(up_proj, grad_pre_up, contract, preferred_element_type=jnp.float32)
    ).astype(jnp.bfloat16)
    back_rows = lax.all_to_all(partial_rows, "expert", split_axis=1, concat_axis=1, tiled=True)
    back_gate = lax.all_to_all(
        slot_gate_grad.reshape(1, slot_count), "expert", split_axis=1, concat_axis=1, tiled=True
    )
    local_sums = lax.dot_general(
        picker_half, back_rows, (((0,), (1,)), ((), ())), preferred_element_type=jnp.float32
    )
    grad_in = lax.psum_scatter(
        local_sums.astype(jnp.bfloat16), "tensor", scatter_dimension=1, tiled=True
    )
    position = jnp.where(occupied, entries, tok_count * top_count)
    gate_sums = (
        jnp.zeros((tok_count * top_count + 1,), jnp.float32).at[position].add(back_gate.reshape(-1))
    )
    grad_gate = gate_sums[:-1].reshape(tok_count, top_count)
    return (grad_in, grad_gate)


NZ, NY, NX, NC = 4, 2, 2, 2


def _pairs(move):
    pairs = []
    for z in range(NZ):
        for y in range(NY):
            for x in range(NX):
                for c in range(NC):
                    tz, ty, tx, tc = move(z, y, x, c)
                    pairs.append((((z * NY + y) * NX + x) * NC + c, ((tz * NY + ty) * NX + tx) * NC + tc))
    return pairs


TO_X = _pairs(lambda z, y, x, c: (z, y, 1 - x, c))
TO_Y = _pairs(lambda z, y, x, c: (z, 1 - y, x, c))
TO_CORE = _pairs(lambda z, y, x, c: (z, y, x, 1 - c))
LEFT = _pairs(lambda z, y, x, c: (z, y, 1 - x, c) if c == 0 else (z, 1 - y, x, c))
RIGHT = _pairs(lambda z, y, x, c: (z, 1 - y, x, c) if c == 0 else (z, y, 1 - x, c))
TO_Z = [_pairs(lambda z, y, x, c, d=d: (z ^ d, y, x, c)) for d in range(NZ)]
CHUNKS = ((0, 2), (1, 3))


def send(value, pairs, name="send"):
    with jax.named_scope(name):
        return lax.ppermute(value, BOTH, pairs)


def after(value, *first):
    return lax.optimization_barrier((value, *first))[0]


def dot_nt(a, b):
    return lax.dot_general(a, b, (((1,), (1,)), ((), ())), preferred_element_type=F32)


def shape_of(shape, dtype):
    return jax.ShapeDtypeStruct(shape, dtype)


HINT = pl.CostEstimate(flops=0, transcendentals=0, bytes_accessed=0)
LARGE = pltpu.CompilerParams(vmem_limit_bytes=48 << 20)


def kernel(name, body, outs, grid, in_specs, out_specs, *args, scratch=()):
    return pl.pallas_call(
        body,
        out_shape=outs,
        grid_spec=pltpu.PrefetchScalarGridSpec(
            num_scalar_prefetch=1, grid=grid, in_specs=in_specs, out_specs=out_specs, scratch_shapes=scratch
        ),
        compiler_params=LARGE,
        cost_estimate=HINT,
        name=name,
    )(*args)


META = 8


def pack_rows(grad_out, slots, gates):
    tokens, quarter = grad_out.shape
    experts = slots.shape[0]
    top_count = gates.shape[0]

    def body(g_ref, s_ref, w_ref, out, choice_ref):
        out[:tokens] = g_ref[...]
        entries = s_ref[...]
        owner = lax.div(entries, top_count)
        choice = (entries - owner * top_count).astype(F32)
        owner = owner.astype(F32)
        gate = w_ref[...].astype(F32)
        square = lax.broadcasted_iota(jnp.int32, (tokens, tokens), 0).astype(F32)
        row = lax.broadcasted_iota(jnp.int32, (META, tokens), 0)
        lane = lax.broadcasted_iota(jnp.int32, (META, tokens), 1).astype(F32)
        number = lax.broadcasted_iota(jnp.int32, (top_count, tokens), 0).astype(F32)
        for e in range(experts):
            hit = jnp.where(square == owner[e : e + 1], 1.0, 0.0).astype(BF16)
            value = jnp.where(row == 0, lane, choice[e : e + 1]).astype(BF16)
            found = dot_nt(value, hit)
            chosen = found[1:2]
            weight = jnp.sum(jnp.where(number == chosen, gate, 0.0), axis=0, keepdims=True)
            choice_ref[e : e + 1, :] = chosen
            out[tokens:, e * tokens : (e + 1) * tokens] = jnp.where(row == 0, found, weight).astype(BF16)

    full = lambda shape: pl.BlockSpec(shape, lambda i: (0, 0))
    return pl.pallas_call(
        body,
        out_shape=[shape_of((tokens + META, quarter), BF16), shape_of((experts, tokens), F32)],
        grid=(1,),
        in_specs=[full(grad_out.shape), full(slots.shape), full(gates.shape)],
        out_specs=[full((tokens + META, quarter)), full((experts, tokens))],
        compiler_params=pltpu.CompilerParams(vmem_limit_bytes=60 << 20),
        cost_estimate=HINT,
        name="pack",
    )(grad_out, slots, gates)


def prepare(expert, block, near, saved_gate, saved_up, chunk):
    tokens = near[0][0].shape[0] - META
    hid = saved_gate.shape[1]
    count = len(chunk)
    low, step = chunk[0], chunk[1] - chunk[0]

    def group(i, e, s):
        return ((e[0] // NY) ^ (low + step * (i % count))) * NY + ((e[0] % NY) ^ (i // count))

    def body(e_ref, s_ref, *refs):
        metas = refs[: 3 * count]
        g_ref, u_ref = refs[3 * count : 3 * count + 2]
        outs = refs[3 * count + 2 :]
        i, c = pl.program_id(0), s_ref[0] % NC
        meta = None
        for k in range(count):
            own, first, second = (m[...].astype(F32) for m in metas[3 * k : 3 * k + 3])
            mine = jnp.where(i // count == 0, own, jnp.where(c == 0, first, second))
            meta = mine if meta is None else jnp.where(i % count == k, mine, meta)
        slots = lax.broadcasted_iota(jnp.int32, (tokens, tokens), 0).astype(F32)
        pick = jnp.where(slots == meta[0:1], 1.0, 0.0).astype(BF16)
        flip = (((0,), (0,)), ((), ()))
        gate_pre = lax.dot_general(pick, g_ref[...], flip, preferred_element_type=F32)
        up_pre = lax.dot_general(pick, u_ref[...], flip, preferred_element_type=F32)
        scale = jnp.transpose(jnp.broadcast_to(meta[1:2], (tokens, tokens)))[:, 0:1]
        activated, derivative = silu_pair(gate_pre)
        outs[0][...] = activated * up_pre
        outs[1][...] = scale * up_pre * derivative
        outs[2][...] = scale * activated

    out = shape_of((NY * count * tokens, hid), F32)
    meta = pl.BlockSpec((META, tokens), lambda i, e, s: (tokens // META, e[0]))
    saved = pl.BlockSpec((tokens, hid), lambda i, e, s: (group(i, e, s), 0))
    spec = pl.BlockSpec((tokens, hid), lambda i, e, s: (i, 0))
    flat = [p for three in near for p in three]
    return pl.pallas_call(
        body,
        out_shape=[out] * 3,
        grid_spec=pltpu.PrefetchScalarGridSpec(
            num_scalar_prefetch=2,
            grid=(NY * count,),
            in_specs=[meta] * len(flat) + [saved, saved],
            out_specs=[spec] * 3,
        ),
        compiler_params=LARGE,
        cost_estimate=HINT,
        name="prepare",
    )(expert, block, *flat, saved_gate, saved_up)


def hidden_parts(block, pieces, down, got):
    tokens, quarter = pieces[0][0].shape[0] - META, pieces[0][0].shape[1]
    hid = down.shape[0]
    count = len(pieces)
    half = count * tokens
    rows = NY * half
    steps = 2
    wide = quarter // steps

    def body(s_ref, *refs):
        near = refs[: 4 * count]
        d_ref, o_ref, mine, theirs, rows_v, w_v, row_sem, w_sem = refs[4 * count :]
        x, c = s_ref[0] // NC, s_ref[0] % NC

        def weight(dx, h, k):
            first = pl.multiple_of((2 * (x ^ dx) + c) * quarter + h * wide, wide)
            source = (d_ref, o_ref)[k].at[:, pl.ds(first, wide)]
            return pltpu.make_async_copy(source, w_v.at[dx, h, pl.ds(k * hid, hid), :], w_sem.at[dx, h, k])

        def piece(i, j, dx, h, dy):
            target = rows_v.at[dx, h, pl.ds(dy * half + i * tokens, tokens), :]
            source = near[4 * i + j].at[pl.ds(0, tokens), pl.ds(h * wide, wide)]
            return pltpu.make_async_copy(source, target, row_sem.at[i, dx, h, dy])

        def begin(dx, h):
            for k in (1, 0):
                weight(dx, h, k).start()
            for i in range(count):
                piece(i, 0 if dx == 0 else 3, dx, h, dx).start()

                @pl.when(c == dx)
                def _(i=i, dx=dx, h=h):
                    piece(i, 1, dx, h, 1 - dx).start()

                @pl.when(c != dx)
                def _(i=i, dx=dx, h=h):
                    piece(i, 2, dx, h, 1 - dx).start()

        order = [(dx, h) for dx in range(NX) for h in range(steps)]
        begin(*order[0])
        begin(*order[1])
        total = None
        for n, (dx, h) in enumerate(order):
            for i in range(count):
                for dy in range(NY):
                    piece(i, 0, dx, h, dy).wait()
            for k in (1, 0):
                weight(dx, h, k).wait()
            if n + 2 < len(order):
                begin(*order[n + 2])
            part = dot_nt(rows_v[dx, h], w_v[dx, h])
            total = part if n == 0 else total + part
        mine[...] = total[:, :hid]
        theirs[...] = total[:, hid:].astype(BF16)

    flat = [p for four in pieces for p in four]
    spec = lambda cols: pl.BlockSpec((rows, cols), lambda i, s: (0, 0))
    return kernel(
        "hidden",
        body,
        [shape_of((rows, hid), F32), shape_of((rows, hid), BF16)],
        (1,),
        [pl.BlockSpec(memory_space=pl.ANY)] * (len(flat) + 2),
        [spec(hid)] * 2,
        block,
        *flat,
        down,
        got,
        scratch=[
            pltpu.VMEM((NX, steps, rows, wide), BF16),
            pltpu.VMEM((NX, steps, 2 * hid, wide), BF16),
            pltpu.SemaphoreType.DMA((count, NX, steps, NY)),
            pltpu.SemaphoreType.DMA((NX, steps, 2)),
        ],
    )


def pre_grads(block, mine, back, factors):
    rows, hid = mine.shape
    half = rows // NY
    count = len(CHUNKS[0])
    tokens = half // count

    def body(s_ref, m_ref, b_ref, f0, f1, f2, h_ref, t_ref):
        bh = m_ref[...] + b_ref[...].astype(F32)
        h_ref[:, :hid] = (bh * f1[...]).astype(BF16)
        h_ref[:, hid:] = (bh * f2[...]).astype(BF16)
        term = jnp.sum(bh * f0[...], axis=1, keepdims=True)
        flat = jnp.transpose(jnp.broadcast_to(term, (half, 128)))
        for i in range(count):
            t_ref[0, i : i + 1, :] = flat[0:1, i * tokens : (i + 1) * tokens]

    outs = [shape_of((rows, 2 * hid), BF16), shape_of((NY, count, tokens), F32)]
    spec = lambda cols: pl.BlockSpec((half, cols), lambda i, s: (i, 0))
    return kernel(
        "pre_grads",
        body,
        outs,
        (NY,),
        [spec(hid)] * 5,
        [spec(2 * hid), pl.BlockSpec((1, count, tokens), lambda i, s: (i, 0, 0))],
        block,
        mine,
        back,
        *factors,
    )


def input_parts(block, mine, theirs, weights, got):
    rows = mine.shape[0] // NY
    hid = mine.shape[1] // 2
    quarter = weights[0].shape[0] // (NX * NC)
    steps = 2
    wide = quarter // steps
    order = [(dx, h) for dx in (1, 0) for h in range(steps)]

    def body(s_ref, m_ref, t_ref, *refs):
        sources = refs[:4]
        outs = refs[4:8]
        side_v, w_v, o_v, side_sem, sem, out_sem = refs[8:]
        x, c = s_ref[0] // NC, s_ref[0] % NC

        def weight(n, j):
            dx, h = order[n]
            first = pl.multiple_of((2 * (x ^ dx) + c) * quarter + h * wide, wide)
            target = w_v.at[n, j // 2, :, pl.ds((j % 2) * hid, hid)]
            return pltpu.make_async_copy(sources[j].at[pl.ds(first, wide), :], target, sem.at[n, j])

        def side(k):
            return pltpu.make_async_copy((m_ref, t_ref)[k], side_v.at[k], side_sem.at[k])

        def give(which, n, dy):
            cols = pl.ds(order[n][1] * wide, wide)
            return pltpu.make_async_copy(o_v.at[n, dy], outs[which].at[:, cols], out_sem.at[n, dy])

        side(0).start()
        for j in range(4):
            weight(0, j).start()
        side(1).start()
        for j in range(4):
            weight(1, j).start()
        side(0).wait()
        for n, (dx, h) in enumerate(order):
            total = None
            for k in range(2):
                for j in (2 * k, 2 * k + 1):
                    weight(n, j).wait()
                if n == 0 and k == 1:
                    side(1).wait()
                part = dot_nt(side_v[k], w_v[n, k])
                total = part if k == 0 else total + part
                for j in (2 * k, 2 * k + 1):
                    if n + 2 < len(order):
                        weight(n + 2, j).start()
            o_v[n, 0] = total[:rows].astype(BF16)
            o_v[n, 1] = total[rows:].astype(BF16)
            give(0 if dx == 1 else 3, n, dx).start()

            @pl.when(c == 1 - dx)
            def _(n=n, dx=dx):
                give(1, n, 1 - dx).start()

            @pl.when(c != 1 - dx)
            def _(n=n, dx=dx):
                give(2, n, 1 - dx).start()

        for n in range(len(order)):
            for dy in range(NY):
                give(0, n, dy).wait()

    far = pl.BlockSpec(memory_space=pl.ANY)
    return kernel(
        "input",
        body,
        [shape_of((rows, quarter), BF16)] * 4,
        (1,),
        [far] * 6,
        [far] * 4,
        block,
        mine,
        theirs,
        *weights,
        *got,
        scratch=[
            pltpu.VMEM((2,) + mine.shape, BF16),
            pltpu.VMEM((len(order), 2, wide, 2 * hid), BF16),
            pltpu.VMEM((len(order), NY, rows, wide), BF16),
            pltpu.SemaphoreType.DMA((2,)),
            pltpu.SemaphoreType.DMA((len(order), 4)),
            pltpu.SemaphoreType.DMA((len(order), NY)),
        ],
    )


def add_pieces(block, base, first, second, types):
    rows, cols = base.shape
    part = rows // len(types)
    wide = cols // 2

    def body(s_ref, b_ref, f_ref, g_ref, *outs):
        for i, out in enumerate(outs):
            s = slice(i * part, (i + 1) * part)
            out[...] = (b_ref[s].astype(F32) + f_ref[s].astype(F32) + g_ref[s].astype(F32)).astype(out.dtype)

    spec = lambda n: pl.BlockSpec((n, wide), lambda i, s: (0, i))
    outs = [shape_of((part, cols), t) for t in types]
    return kernel("add", body, outs, (2,), [spec(rows)] * 3, [spec(part)] * len(outs), block, base, first, second)


def add_corner(block, base, corner):
    rows, cols = base.shape

    def body(s_ref, b_ref, c_ref, out):
        out[...] = (b_ref[...].astype(F32) + c_ref[...].astype(F32)).astype(BF16)

    spec = pl.BlockSpec((rows, cols // 2), lambda i, s: (0, i))
    return kernel("corner", body, shape_of(base.shape, BF16), (2,), [spec] * 2, spec, block, base, corner)


def last_sum(block, keep, parts, out_type):
    def body(s_ref, k_ref, *refs):
        total = k_ref[...]
        for ref in refs[:-1]:
            total = total + ref[...].astype(F32)
        refs[-1][...] = total.astype(out_type)

    spec = pl.BlockSpec(keep.shape, lambda i, s: (0, 0))
    return kernel(
        "last", body, shape_of(keep.shape, out_type), (1,), [spec] * (1 + len(parts)), spec, block, keep, *parts
    )


def dense_local(grad_out, gate_weights, slot_lists, saved_gate, saved_up, w_gate, w_up, w_down):
    tokens, quarter = grad_out.shape
    experts = slot_lists.shape[1]
    top_count = gate_weights.shape[1]
    expert = lax.axis_index("expert")
    block = lax.axis_index("tensor")
    z, y = expert // NY, expert % NY
    at_expert, at_block = expert.reshape(1), block.reshape(1)

    down, gate_w, up_w = w_down[0], w_gate[0], w_up[0]
    near, far = CHUNKS
    own, choice_of = pack_rows(grad_out, slot_lists[0], gate_weights.T)

    z2, z1 = send(own, TO_Z[2], "z2"), send(own, TO_Z[1], "z1")
    first0, second0 = send(own, RIGHT, "first0"), send(own, LEFT, "second0")
    got_down = send(down, TO_CORE, "weights")

    z2, z1, first0, second0, got_down, gate_w_, up_w_ = lax.optimization_barrier(
        (z2, z1, first0, second0, got_down, gate_w, up_w)
    )
    first2, second2 = send(z2, RIGHT, "first2"), send(z2, LEFT, "second2")
    third0 = send(first0, LEFT, "third0")
    z3 = send(z2, TO_Z[1], "z3")
    got_gate = send(gate_w_, TO_CORE, "weights")

    z1, z3, first2, second2, third0, got_gate, up_w_ = lax.optimization_barrier(
        (z1, z3, first2, second2, third0, got_gate, up_w_)
    )
    got_up = send(up_w_, TO_CORE, "weights")
    third2 = send(first2, LEFT, "third2")
    first1, second1 = send(z1, RIGHT, "first1"), send(z1, LEFT, "second1")
    first3 = send(z3, RIGHT, "first3")
    saved = saved_gate[0], saved_up[0]
    factors_a = prepare(
        at_expert, at_block, [(own, first0, second0), (z2, first2, second2)], *saved, near
    )
    place = after(at_block, factors_a[0])

    weights, got = (gate_w, up_w), (got_gate, got_up)

    def stage_corner(place, chunk, left, corner):
        value = add_corner(place, left, corner)
        return send(value, RIGHT, f"r_left{chunk[0]}"), value

    def stage_add(place, chunk, base, right, left):
        types = [F32 if d == 0 else BF16 for d in chunk]
        totals = add_pieces(place, base, right, left, types)
        return {d: t if d == 0 else send(t, TO_Z[d], f"r_z{d}") for d, t in zip(chunk, totals)}, totals[0]

    mine, theirs = hidden_parts(
        place, [(own, first0, second0, third0), (z2, first2, second2, third2)], down, got_down
    )
    theirs, first1, second1, got_up, first3 = lax.optimization_barrier((theirs, first1, second1, got_up, first3))
    back = send(theirs, TO_CORE, "swap_bh0")
    second3 = send(z3, LEFT, "second3")
    third3 = send(first3, LEFT, "third3")
    third1 = send(first1, LEFT, "third1")
    mine, term_a = pre_grads(after(at_block, mine), mine, back, factors_a)
    theirs = send(mine, TO_CORE, "swap_h0")
    place = at_block
    corner_a, right_a, left_a, base_a = input_parts(place, mine, theirs, weights, got)
    place = after(at_block, base_a)
    corner_a, right_a = send(corner_a, LEFT, "r_corner0"), send(right_a, LEFT, "r_right0")

    factors_b = prepare(
        at_expert, place, [(z1, first1, second1), (z3, first3, second3)], *saved, far
    )
    place = after(at_block, factors_b[0])
    mine, theirs = hidden_parts(
        place, [(z1, first1, second1, third1), (z3, first3, second3, third3)], down, got_down
    )
    back = send(theirs, TO_CORE, "swap_bh1")
    place = after(at_block, mine)
    left_a, value = stage_corner(place, near, left_a, corner_a)
    place = after(at_block, value)
    mine, term_b = pre_grads(place, mine, back, factors_b)
    theirs = send(mine, TO_CORE, "swap_h1")
    place = at_block
    corner_b, right_b, left_b, base_b = input_parts(place, mine, theirs, weights, got)
    place = after(at_block, base_b)
    corner_b, right_b = send(corner_b, LEFT, "r_corner1"), send(right_b, LEFT, "r_right1")
    sums, value = stage_add(place, near, base_a, right_a, left_a)
    left_b, value = stage_corner(after(at_block, value), far, left_b, corner_b)
    early = sums[2]
    more, kept = stage_add(after(at_block, value), far, base_b, right_b, left_b)
    sums.update(more)
    grad_in = last_sum(at_block, sums[0], [sums[d] for d in (2, 1, 3)], BF16)

    terms = {d: t[:, i] for c, t in ((near, term_a), (far, term_b)) for i, d in enumerate(c)}
    term = jnp.stack([terms[d] for d in range(NZ)], axis=1)
    term = term + send(term, TO_CORE, "t_core")
    term = term + send(after(term, base_b), TO_X, "t_x")
    term = after(term, value)
    term = jnp.stack([term[0], send(term[1], TO_Y, "t_y")], axis=1)
    term = after(term, kept, early)
    slots = [term[0]] + [send(term[d], TO_Z[d], f"t_z{d}") for d in range(1, NZ)]
    slot_grad = jnp.zeros((experts, tokens), F32)
    ids = jnp.arange(experts, dtype=jnp.int32)
    for d in range(NZ):
        for dy in range(NY):
            source = (z ^ d) * NY + (y ^ dy)
            slot_grad = jnp.where((ids == source)[:, None], slots[d][dy][None], slot_grad)
    choice_ids = jnp.arange(top_count, dtype=F32)
    chosen = choice_of[:, :, None] == choice_ids[None, None, :]
    grad_gate = jnp.sum(jnp.where(chosen, slot_grad[:, :, None], 0.0), axis=0)
    return (grad_in, grad_gate)


def local(grad_out, gate_weights, slot_lists, *rest):
    tokens = grad_out.shape[0]
    _, experts, capacity = slot_lists.shape
    dense = experts == gate_weights.shape[1] == NZ * NY and capacity == tokens
    dense = dense and lax.axis_size("expert") == NZ * NY and lax.axis_size("tensor") == NX * NC
    program = dense_local if dense else routed_local
    return program(grad_out, gate_weights, slot_lists, *rest)


def solution(mesh):
    in_specs = (
        P("expert", "tensor"),
        P("expert", None),
        P("expert", None, None),
        P("expert", None, "tensor"),
        P("expert", None, "tensor"),
        P("expert", None, "tensor"),
        P("expert", None, "tensor"),
        P("expert", "tensor", None),
    )
    out_specs = (P("expert", "tensor"), P("expert", None))
    return jax.shard_map(local, mesh=mesh, in_specs=in_specs, out_specs=out_specs, check_vma=False)
```

```python
import jax
import jax.numpy as jnp
from jax import lax
from jax.experimental import pallas as pl
from jax.experimental.pallas import tpu as pltpu
from jax.sharding import PartitionSpec as P

BOTH = ("expert", "tensor")
F32 = jnp.float32
BF16 = jnp.bfloat16


def silu_pair(pre_act):
    sigma = jax.nn.sigmoid(pre_act)
    return (pre_act * sigma, sigma * (1.0 + pre_act * (1.0 - sigma)))


def routed_local(grad_out, gate_weights, slot_lists, saved_gate, saved_up, w_gate, w_up, w_down):
    slot_table = slot_lists[0]
    experts, capacity = slot_table.shape
    tok_count, quarter = grad_out.shape
    top_count = gate_weights.shape[1]
    entries = slot_table.reshape(-1)
    occupied = entries >= 0
    owner_token = jnp.where(occupied, entries // top_count, -1)
    picker = owner_token[:, None] == jnp.arange(tok_count, dtype=jnp.int32)[None, :]
    picker_half = picker.astype(jnp.bfloat16)
    send_rows = jnp.dot(picker_half, grad_out, preferred_element_type=jnp.float32).astype(
        jnp.bfloat16
    )
    send_gate = jnp.where(
        occupied, gate_weights.reshape(-1)[jnp.maximum(entries, 0)], jnp.zeros((), jnp.bfloat16)
    )
    got_rows, got_gate = (
        lax.all_to_all(
            send_rows.reshape(experts, capacity, quarter),
            "expert",
            split_axis=0,
            concat_axis=0,
            tiled=True,
        ),
        lax.all_to_all(
            send_gate.reshape(experts, capacity), "expert", split_axis=0, concat_axis=0, tiled=True
        ),
    )
    slot_count = got_rows.shape[0] * capacity
    routed = got_rows.reshape(slot_count, quarter)
    down_proj = w_down[0]
    contract = (((1,), (1,)), ((), ()))
    back_hidden = lax.dot_general(
        lax.all_gather(routed, "tensor", axis=1, tiled=True),
        down_proj,
        contract,
        preferred_element_type=jnp.float32,
    )
    gate_pre = saved_gate[0].astype(jnp.float32)
    up_pre = saved_up[0].astype(jnp.float32)
    activated, derivative = silu_pair(gate_pre)
    hidden = activated * up_pre
    slot_gate_grad = lax.psum(jnp.sum(back_hidden * hidden, axis=1), "tensor")
    scaled = got_gate.reshape(slot_count).astype(jnp.float32)[:, None] * back_hidden
    grad_pre_gate = (scaled * up_pre * derivative).astype(jnp.bfloat16)
    grad_pre_up = (scaled * activated).astype(jnp.bfloat16)
    gate_proj = w_gate[0]
    up_proj = w_up[0]
    partial_rows = lax.dot_general(
        gate_proj, grad_pre_gate, contract, preferred_element_type=jnp.float32
    )
    partial_rows = (
        partial_rows
        + lax.dot_general(up_proj, grad_pre_up, contract, preferred_element_type=jnp.float32)
    ).astype(jnp.bfloat16)
    back_rows = lax.all_to_all(partial_rows, "expert", split_axis=1, concat_axis=1, tiled=True)
    back_gate = lax.all_to_all(
        slot_gate_grad.reshape(1, slot_count), "expert", split_axis=1, concat_axis=1, tiled=True
    )
    local_sums = lax.dot_general(
        picker_half, back_rows, (((0,), (1,)), ((), ())), preferred_element_type=jnp.float32
    )
    grad_in = lax.psum_scatter(
        local_sums.astype(jnp.bfloat16), "tensor", scatter_dimension=1, tiled=True
    )
    position = jnp.where(occupied, entries, tok_count * top_count)
    gate_sums = (
        jnp.zeros((tok_count * top_count + 1,), jnp.float32).at[position].add(back_gate.reshape(-1))
    )
    grad_gate = gate_sums[:-1].reshape(tok_count, top_count)
    return (grad_in, grad_gate)


NZ, NY, NX, NC = 4, 2, 2, 2


def _pairs(move):
    pairs = []
    for z in range(NZ):
        for y in range(NY):
            for x in range(NX):
                for c in range(NC):
                    tz, ty, tx, tc = move(z, y, x, c)
                    pairs.append((((z * NY + y) * NX + x) * NC + c, ((tz * NY + ty) * NX + tx) * NC + tc))
    return pairs


TO_X = _pairs(lambda z, y, x, c: (z, y, 1 - x, c))
TO_Y = _pairs(lambda z, y, x, c: (z, 1 - y, x, c))
TO_CORE = _pairs(lambda z, y, x, c: (z, y, x, 1 - c))
LEFT = _pairs(lambda z, y, x, c: (z, y, 1 - x, c) if c == 0 else (z, 1 - y, x, c))
RIGHT = _pairs(lambda z, y, x, c: (z, 1 - y, x, c) if c == 0 else (z, y, 1 - x, c))
TO_Z = [_pairs(lambda z, y, x, c, d=d: (z ^ d, y, x, c)) for d in range(NZ)]
CHUNKS = ((0, 2), (1, 3))


def send(value, pairs, name="send"):
    with jax.named_scope(name):
        return lax.ppermute(value, BOTH, pairs)


def after(value, *first):
    return lax.optimization_barrier((value, *first))[0]


def dot_nt(a, b):
    return lax.dot_general(a, b, (((1,), (1,)), ((), ())), preferred_element_type=F32)


def shape_of(shape, dtype):
    return jax.ShapeDtypeStruct(shape, dtype)


HINT = pl.CostEstimate(flops=0, transcendentals=0, bytes_accessed=0)
LARGE = pltpu.CompilerParams(vmem_limit_bytes=48 << 20)


def kernel(name, body, outs, grid, in_specs, out_specs, *args, scratch=()):
    return pl.pallas_call(
        body,
        out_shape=outs,
        grid_spec=pltpu.PrefetchScalarGridSpec(
            num_scalar_prefetch=1, grid=grid, in_specs=in_specs, out_specs=out_specs, scratch_shapes=scratch
        ),
        compiler_params=LARGE,
        cost_estimate=HINT,
        name=name,
    )(*args)


META = 8


def pack_rows(grad_out, slots, gates):
    tokens, quarter = grad_out.shape
    experts = slots.shape[0]
    top_count = gates.shape[0]

    def body(g_ref, s_ref, w_ref, out, choice_ref):
        out[:tokens] = g_ref[...]
        entries = s_ref[...]
        owner = lax.div(entries, top_count)
        choice = (entries - owner * top_count).astype(F32)
        owner = owner.astype(F32)
        gate = w_ref[...].astype(F32)
        square = lax.broadcasted_iota(jnp.int32, (tokens, tokens), 0).astype(F32)
        row = lax.broadcasted_iota(jnp.int32, (META, tokens), 0)
        lane = lax.broadcasted_iota(jnp.int32, (META, tokens), 1).astype(F32)
        number = lax.broadcasted_iota(jnp.int32, (top_count, tokens), 0).astype(F32)
        for e in range(experts):
            hit = jnp.where(square == owner[e : e + 1], 1.0, 0.0).astype(BF16)
            value = jnp.where(row == 0, lane, choice[e : e + 1]).astype(BF16)
            found = dot_nt(value, hit)
            chosen = found[1:2]
            weight = jnp.sum(jnp.where(number == chosen, gate, 0.0), axis=0, keepdims=True)
            choice_ref[e : e + 1, :] = chosen
            out[tokens:, e * tokens : (e + 1) * tokens] = jnp.where(row == 0, found, weight).astype(BF16)

    full = lambda shape: pl.BlockSpec(shape, lambda i: (0, 0))
    return pl.pallas_call(
        body,
        out_shape=[shape_of((tokens + META, quarter), BF16), shape_of((experts, tokens), F32)],
        grid=(1,),
        in_specs=[full(grad_out.shape), full(slots.shape), full(gates.shape)],
        out_specs=[full((tokens + META, quarter)), full((experts, tokens))],
        compiler_params=pltpu.CompilerParams(vmem_limit_bytes=60 << 20),
        cost_estimate=HINT,
        name="pack",
    )(grad_out, slots, gates)


def prepare(expert, block, near, saved_gate, saved_up, chunk):
    tokens = near[0][0].shape[0] - META
    hid = saved_gate.shape[1]
    count = len(chunk)
    low, step = chunk[0], chunk[1] - chunk[0]

    def group(i, e, s):
        return ((e[0] // NY) ^ (low + step * (i % count))) * NY + ((e[0] % NY) ^ (i // count))

    def body(e_ref, s_ref, *refs):
        metas = refs[: 3 * count]
        g_ref, u_ref = refs[3 * count : 3 * count + 2]
        outs = refs[3 * count + 2 :]
        i, c = pl.program_id(0), s_ref[0] % NC
        meta = None
        for k in range(count):
            own, first, second = (m[...].astype(F32) for m in metas[3 * k : 3 * k + 3])
            mine = jnp.where(i // count == 0, own, jnp.where(c == 0, first, second))
            meta = mine if meta is None else jnp.where(i % count == k, mine, meta)
        slots = lax.broadcasted_iota(jnp.int32, (tokens, tokens), 0).astype(F32)
        pick = jnp.where(slots == meta[0:1], 1.0, 0.0).astype(BF16)
        flip = (((0,), (0,)), ((), ()))
        gate_pre = lax.dot_general(pick, g_ref[...], flip, preferred_element_type=F32)
        up_pre = lax.dot_general(pick, u_ref[...], flip, preferred_element_type=F32)
        scale = jnp.transpose(jnp.broadcast_to(meta[1:2], (tokens, tokens)))[:, 0:1]
        activated, derivative = silu_pair(gate_pre)
        outs[0][...] = activated * up_pre
        outs[1][...] = scale * up_pre * derivative
        outs[2][...] = scale * activated

    out = shape_of((NY * count * tokens, hid), F32)
    meta = pl.BlockSpec((META, tokens), lambda i, e, s: (tokens // META, e[0]))
    saved = pl.BlockSpec((tokens, hid), lambda i, e, s: (group(i, e, s), 0))
    spec = pl.BlockSpec((tokens, hid), lambda i, e, s: (i, 0))
    flat = [p for three in near for p in three]
    return pl.pallas_call(
        body,
        out_shape=[out] * 3,
        grid_spec=pltpu.PrefetchScalarGridSpec(
            num_scalar_prefetch=2,
            grid=(NY * count,),
            in_specs=[meta] * len(flat) + [saved, saved],
            out_specs=[spec] * 3,
        ),
        compiler_params=LARGE,
        cost_estimate=HINT,
        name="prepare",
    )(expert, block, *flat, saved_gate, saved_up)


def hidden_parts(block, pieces, down, got):
    tokens, quarter = pieces[0][0].shape[0] - META, pieces[0][0].shape[1]
    hid = down.shape[0]
    count = len(pieces)
    half = count * tokens
    rows = NY * half
    steps = 2
    wide = quarter // steps

    def body(s_ref, *refs):
        near = refs[: 4 * count]
        d_ref, o_ref, mine, theirs, rows_v, w_v, row_sem, w_sem = refs[4 * count :]
        x, c = s_ref[0] // NC, s_ref[0] % NC

        def weight(dx, h, k):
            first = pl.multiple_of((2 * (x ^ dx) + c) * quarter + h * wide, wide)
            source = (d_ref, o_ref)[k].at[:, pl.ds(first, wide)]
            return pltpu.make_async_copy(source, w_v.at[dx, h, pl.ds(k * hid, hid), :], w_sem.at[dx, h, k])

        def piece(i, j, dx, h, dy):
            target = rows_v.at[dx, h, pl.ds(dy * half + i * tokens, tokens), :]
            source = near[4 * i + j].at[pl.ds(0, tokens), pl.ds(h * wide, wide)]
            return pltpu.make_async_copy(source, target, row_sem.at[i, dx, h, dy])

        def begin(dx, h):
            for k in (1, 0):
                weight(dx, h, k).start()
            for i in range(count):
                piece(i, 0 if dx == 0 else 3, dx, h, dx).start()

                @pl.when(c == dx)
                def _(i=i, dx=dx, h=h):
                    piece(i, 1, dx, h, 1 - dx).start()

                @pl.when(c != dx)
                def _(i=i, dx=dx, h=h):
                    piece(i, 2, dx, h, 1 - dx).start()

        order = [(dx, h) for dx in range(NX) for h in range(steps)]
        begin(*order[0])
        begin(*order[1])
        total = None
        for n, (dx, h) in enumerate(order):
            for i in range(count):
                for dy in range(NY):
                    piece(i, 0, dx, h, dy).wait()
            for k in (1, 0):
                weight(dx, h, k).wait()
            if n + 2 < len(order):
                begin(*order[n + 2])
            part = dot_nt(rows_v[dx, h], w_v[dx, h])
            total = part if n == 0 else total + part
        mine[...] = total[:, :hid]
        theirs[...] = total[:, hid:].astype(BF16)

    flat = [p for four in pieces for p in four]
    spec = lambda cols: pl.BlockSpec((rows, cols), lambda i, s: (0, 0))
    return kernel(
        "hidden",
        body,
        [shape_of((rows, hid), F32), shape_of((rows, hid), BF16)],
        (1,),
        [pl.BlockSpec(memory_space=pl.ANY)] * (len(flat) + 2),
        [spec(hid)] * 2,
        block,
        *flat,
        down,
        got,
        scratch=[
            pltpu.VMEM((NX, steps, rows, wide), BF16),
            pltpu.VMEM((NX, steps, 2 * hid, wide), BF16),
            pltpu.SemaphoreType.DMA((count, NX, steps, NY)),
            pltpu.SemaphoreType.DMA((NX, steps, 2)),
        ],
    )


def pre_grads(block, mine, back, factors):
    rows, hid = mine.shape
    half = rows // NY
    count = len(CHUNKS[0])
    tokens = half // count

    def body(s_ref, m_ref, b_ref, f0, f1, f2, h_ref, t_ref):
        bh = m_ref[...] + b_ref[...].astype(F32)
        h_ref[:, :hid] = (bh * f1[...]).astype(BF16)
        h_ref[:, hid:] = (bh * f2[...]).astype(BF16)
        term = jnp.sum(bh * f0[...], axis=1, keepdims=True)
        flat = jnp.transpose(jnp.broadcast_to(term, (half, 128)))
        for i in range(count):
            t_ref[0, i : i + 1, :] = flat[0:1, i * tokens : (i + 1) * tokens]

    outs = [shape_of((rows, 2 * hid), BF16), shape_of((NY, count, tokens), F32)]
    spec = lambda cols: pl.BlockSpec((half, cols), lambda i, s: (i, 0))
    return kernel(
        "pre_grads",
        body,
        outs,
        (NY,),
        [spec(hid)] * 5,
        [spec(2 * hid), pl.BlockSpec((1, count, tokens), lambda i, s: (i, 0, 0))],
        block,
        mine,
        back,
        *factors,
    )


def input_parts(block, mine, theirs, weights, got):
    rows = mine.shape[0] // NY
    hid = mine.shape[1] // 2
    quarter = weights[0].shape[0] // (NX * NC)
    steps = 2
    wide = quarter // steps
    order = [(dx, h) for dx in (1, 0) for h in range(steps)]

    def body(s_ref, m_ref, t_ref, *refs):
        sources = refs[:4]
        outs = refs[4:8]
        side_v, w_v, o_v, side_sem, sem, out_sem = refs[8:]
        x, c = s_ref[0] // NC, s_ref[0] % NC

        def weight(n, j):
            dx, h = order[n]
            first = pl.multiple_of((2 * (x ^ dx) + c) * quarter + h * wide, wide)
            target = w_v.at[n, j // 2, :, pl.ds((j % 2) * hid, hid)]
            return pltpu.make_async_copy(sources[j].at[pl.ds(first, wide), :], target, sem.at[n, j])

        def side(k):
            return pltpu.make_async_copy((m_ref, t_ref)[k], side_v.at[k], side_sem.at[k])

        def give(which, n, dy):
            cols = pl.ds(order[n][1] * wide, wide)
            return pltpu.make_async_copy(o_v.at[n, dy], outs[which].at[:, cols], out_sem.at[n, dy])

        side(0).start()
        for j in range(4):
            weight(0, j).start()
        side(1).start()
        for j in range(4):
            weight(1, j).start()
        side(0).wait()
        for n, (dx, h) in enumerate(order):
            total = None
            for k in range(2):
                for j in (2 * k, 2 * k + 1):
                    weight(n, j).wait()
                if n == 0 and k == 1:
                    side(1).wait()
                part = dot_nt(side_v[k], w_v[n, k])
                total = part if k == 0 else total + part
                for j in (2 * k, 2 * k + 1):
                    if n + 2 < len(order):
                        weight(n + 2, j).start()
            o_v[n, 0] = total[:rows].astype(BF16)
            o_v[n, 1] = total[rows:].astype(BF16)
            give(0 if dx == 1 else 3, n, dx).start()

            @pl.when(c == 1 - dx)
            def _(n=n, dx=dx):
                give(1, n, 1 - dx).start()

            @pl.when(c != 1 - dx)
            def _(n=n, dx=dx):
                give(2, n, 1 - dx).start()

        for n in range(len(order)):
            for dy in range(NY):
                give(0, n, dy).wait()

    far = pl.BlockSpec(memory_space=pl.ANY)
    return kernel(
        "input",
        body,
        [shape_of((rows, quarter), BF16)] * 4,
        (1,),
        [far] * 6,
        [far] * 4,
        block,
        mine,
        theirs,
        *weights,
        *got,
        scratch=[
            pltpu.VMEM((2,) + mine.shape, BF16),
            pltpu.VMEM((len(order), 2, wide, 2 * hid), BF16),
            pltpu.VMEM((len(order), NY, rows, wide), BF16),
            pltpu.SemaphoreType.DMA((2,)),
            pltpu.SemaphoreType.DMA((len(order), 4)),
            pltpu.SemaphoreType.DMA((len(order), NY)),
        ],
    )


def add_pieces(block, base, first, second, types):
    rows, cols = base.shape
    part = rows // len(types)
    wide = cols

    def body(s_ref, b_ref, f_ref, g_ref, *outs):
        for i, out in enumerate(outs):
            s = slice(i * part, (i + 1) * part)
            out[...] = (b_ref[s].astype(F32) + f_ref[s].astype(F32) + g_ref[s].astype(F32)).astype(out.dtype)

    spec = lambda n: pl.BlockSpec((n, wide), lambda i, s: (0, i))
    outs = [shape_of((part, cols), t) for t in types]
    return kernel("add", body, outs, (1,), [spec(rows)] * 3, [spec(part)] * len(outs), block, base, first, second)


def add_corner(block, base, corner):
    rows, cols = base.shape

    def body(s_ref, b_ref, c_ref, out):
        out[...] = (b_ref[...].astype(F32) + c_ref[...].astype(F32)).astype(BF16)

    spec = pl.BlockSpec((rows, cols), lambda i, s: (0, i))
    return kernel("corner", body, shape_of(base.shape, BF16), (1,), [spec] * 2, spec, block, base, corner)


def last_sum(block, keep, parts, out_type):
    def body(s_ref, k_ref, *refs):
        total = k_ref[...]
        for ref in refs[:-1]:
            total = total + ref[...].astype(F32)
        refs[-1][...] = total.astype(out_type)

    spec = pl.BlockSpec(keep.shape, lambda i, s: (0, 0))
    return kernel(
        "last", body, shape_of(keep.shape, out_type), (1,), [spec] * (1 + len(parts)), spec, block, keep, *parts
    )


def dense_local(grad_out, gate_weights, slot_lists, saved_gate, saved_up, w_gate, w_up, w_down):
    tokens, quarter = grad_out.shape
    experts = slot_lists.shape[1]
    top_count = gate_weights.shape[1]
    expert = lax.axis_index("expert")
    block = lax.axis_index("tensor")
    z, y = expert // NY, expert % NY
    at_expert, at_block = expert.reshape(1), block.reshape(1)

    down, gate_w, up_w = w_down[0], w_gate[0], w_up[0]
    near, far = CHUNKS
    own, choice_of = pack_rows(grad_out, slot_lists[0], gate_weights.T)

    z2, z1 = send(own, TO_Z[2], "z2"), send(own, TO_Z[1], "z1")
    first0, second0 = send(own, RIGHT, "first0"), send(own, LEFT, "second0")
    got_down = send(down, TO_CORE, "weights")

    z2, z1, first0, second0, got_down, gate_w_, up_w_ = lax.optimization_barrier(
        (z2, z1, first0, second0, got_down, gate_w, up_w)
    )
    first2, second2 = send(z2, RIGHT, "first2"), send(z2, LEFT, "second2")
    third0 = send(first0, LEFT, "third0")
    z3 = send(z2, TO_Z[1], "z3")
    got_gate = send(gate_w_, TO_CORE, "weights")

    z1, z3, first2, second2, third0, got_gate, up_w_ = lax.optimization_barrier(
        (z1, z3, first2, second2, third0, got_gate, up_w_)
    )
    got_up = send(up_w_, TO_CORE, "weights")
    third2 = send(first2, LEFT, "third2")
    first1, second1 = send(z1, RIGHT, "first1"), send(z1, LEFT, "second1")
    first3 = send(z3, RIGHT, "first3")
    saved = saved_gate[0], saved_up[0]
    factors_a = prepare(
        at_expert, at_block, [(own, first0, second0), (z2, first2, second2)], *saved, near
    )
    place = after(at_block, factors_a[0])

    weights, got = (gate_w, up_w), (got_gate, got_up)

    def stage_corner(place, chunk, left, corner):
        value = add_corner(place, left, corner)
        return send(value, RIGHT, f"r_left{chunk[0]}"), value

    def stage_add(place, chunk, base, right, left):
        types = [F32 if d == 0 else BF16 for d in chunk]
        totals = add_pieces(place, base, right, left, types)
        return {d: t if d == 0 else send(t, TO_Z[d], f"r_z{d}") for d, t in zip(chunk, totals)}, totals[0]

    mine, theirs = hidden_parts(
        place, [(own, first0, second0, third0), (z2, first2, second2, third2)], down, got_down
    )
    theirs, first1, second1, got_up, first3 = lax.optimization_barrier((theirs, first1, second1, got_up, first3))
    back = send(theirs, TO_CORE, "swap_bh0")
    second3 = send(z3, LEFT, "second3")
    third3 = send(first3, LEFT, "third3")
    third1 = send(first1, LEFT, "third1")
    mine, term_a = pre_grads(after(at_block, mine), mine, back, factors_a)
    theirs = send(mine, TO_CORE, "swap_h0")
    place = at_block
    corner_a, right_a, left_a, base_a = input_parts(place, mine, theirs, weights, got)
    place = after(at_block, base_a)
    corner_a, right_a = send(corner_a, LEFT, "r_corner0"), send(right_a, LEFT, "r_right0")

    factors_b = prepare(
        at_expert, place, [(z1, first1, second1), (z3, first3, second3)], *saved, far
    )
    place = after(at_block, factors_b[0])
    mine, theirs = hidden_parts(
        place, [(z1, first1, second1, third1), (z3, first3, second3, third3)], down, got_down
    )
    back = send(theirs, TO_CORE, "swap_bh1")
    place = after(at_block, mine)
    left_a, value = stage_corner(place, near, left_a, corner_a)
    place = after(at_block, value)
    mine, term_b = pre_grads(place, mine, back, factors_b)
    theirs = send(mine, TO_CORE, "swap_h1")
    place = at_block
    corner_b, right_b, left_b, base_b = input_parts(place, mine, theirs, weights, got)
    place = after(at_block, base_b)
    corner_b, right_b = send(corner_b, LEFT, "r_corner1"), send(right_b, LEFT, "r_right1")
    sums, value = stage_add(place, near, base_a, right_a, left_a)
    left_b, value = stage_corner(after(at_block, value), far, left_b, corner_b)
    early = sums[2]
    more, kept = stage_add(after(at_block, value), far, base_b, right_b, left_b)
    sums.update(more)
    grad_in = last_sum(at_block, sums[0], [sums[d] for d in (2, 1, 3)], BF16)

    terms = {d: t[:, i] for c, t in ((near, term_a), (far, term_b)) for i, d in enumerate(c)}
    term = jnp.stack([terms[d] for d in range(NZ)], axis=1)
    term = term + send(term, TO_CORE, "t_core")
    term = term + send(after(term, base_b), TO_X, "t_x")
    term = after(term, value)
    term = jnp.stack([term[0], send(term[1], TO_Y, "t_y")], axis=1)
    term = after(term, kept, early)
    slots = [term[0]] + [send(term[d], TO_Z[d], f"t_z{d}") for d in range(1, NZ)]
    slot_grad = jnp.zeros((experts, tokens), F32)
    ids = jnp.arange(experts, dtype=jnp.int32)
    for d in range(NZ):
        for dy in range(NY):
            source = (z ^ d) * NY + (y ^ dy)
            slot_grad = jnp.where((ids == source)[:, None], slots[d][dy][None], slot_grad)
    choice_ids = jnp.arange(top_count, dtype=F32)
    chosen = choice_of[:, :, None] == choice_ids[None, None, :]
    grad_gate = jnp.sum(jnp.where(chosen, slot_grad[:, :, None], 0.0), axis=0)
    return (grad_in, grad_gate)


def local(grad_out, gate_weights, slot_lists, *rest):
    tokens = grad_out.shape[0]
    _, experts, capacity = slot_lists.shape
    dense = experts == gate_weights.shape[1] == NZ * NY and capacity == tokens
    dense = dense and lax.axis_size("expert") == NZ * NY and lax.axis_size("tensor") == NX * NC
    program = dense_local if dense else routed_local
    return program(grad_out, gate_weights, slot_lists, *rest)


def solution(mesh):
    in_specs = (
        P("expert", "tensor"),
        P("expert", None),
        P("expert", None, None),
        P("expert", None, "tensor"),
        P("expert", None, "tensor"),
        P("expert", None, "tensor"),
        P("expert", None, "tensor"),
        P("expert", "tensor", None),
    )
    out_specs = (P("expert", "tensor"), P("expert", None))
    return jax.shard_map(local, mesh=mesh, in_specs=in_specs, out_specs=out_specs, check_vma=False)
```

```python
import jax
import jax.numpy as jnp
from jax import lax
from jax.experimental import pallas as pl
from jax.experimental.pallas import tpu as pltpu
from jax.sharding import PartitionSpec as P

BOTH = ("expert", "tensor")
F32 = jnp.float32
BF16 = jnp.bfloat16


def silu_pair(pre_act):
    sigma = jax.nn.sigmoid(pre_act)
    return (pre_act * sigma, sigma * (1.0 + pre_act * (1.0 - sigma)))


def routed_local(grad_out, gate_weights, slot_lists, saved_gate, saved_up, w_gate, w_up, w_down):
    slot_table = slot_lists[0]
    experts, capacity = slot_table.shape
    tok_count, quarter = grad_out.shape
    top_count = gate_weights.shape[1]
    entries = slot_table.reshape(-1)
    occupied = entries >= 0
    owner_token = jnp.where(occupied, entries // top_count, -1)
    picker = owner_token[:, None] == jnp.arange(tok_count, dtype=jnp.int32)[None, :]
    picker_half = picker.astype(jnp.bfloat16)
    send_rows = jnp.dot(picker_half, grad_out, preferred_element_type=jnp.float32).astype(
        jnp.bfloat16
    )
    send_gate = jnp.where(
        occupied, gate_weights.reshape(-1)[jnp.maximum(entries, 0)], jnp.zeros((), jnp.bfloat16)
    )
    got_rows, got_gate = (
        lax.all_to_all(
            send_rows.reshape(experts, capacity, quarter),
            "expert",
            split_axis=0,
            concat_axis=0,
            tiled=True,
        ),
        lax.all_to_all(
            send_gate.reshape(experts, capacity), "expert", split_axis=0, concat_axis=0, tiled=True
        ),
    )
    slot_count = got_rows.shape[0] * capacity
    routed = got_rows.reshape(slot_count, quarter)
    down_proj = w_down[0]
    contract = (((1,), (1,)), ((), ()))
    back_hidden = lax.dot_general(
        lax.all_gather(routed, "tensor", axis=1, tiled=True),
        down_proj,
        contract,
        preferred_element_type=jnp.float32,
    )
    gate_pre = saved_gate[0].astype(jnp.float32)
    up_pre = saved_up[0].astype(jnp.float32)
    activated, derivative = silu_pair(gate_pre)
    hidden = activated * up_pre
    slot_gate_grad = lax.psum(jnp.sum(back_hidden * hidden, axis=1), "tensor")
    scaled = got_gate.reshape(slot_count).astype(jnp.float32)[:, None] * back_hidden
    grad_pre_gate = (scaled * up_pre * derivative).astype(jnp.bfloat16)
    grad_pre_up = (scaled * activated).astype(jnp.bfloat16)
    gate_proj = w_gate[0]
    up_proj = w_up[0]
    partial_rows = lax.dot_general(
        gate_proj, grad_pre_gate, contract, preferred_element_type=jnp.float32
    )
    partial_rows = (
        partial_rows
        + lax.dot_general(up_proj, grad_pre_up, contract, preferred_element_type=jnp.float32)
    ).astype(jnp.bfloat16)
    back_rows = lax.all_to_all(partial_rows, "expert", split_axis=1, concat_axis=1, tiled=True)
    back_gate = lax.all_to_all(
        slot_gate_grad.reshape(1, slot_count), "expert", split_axis=1, concat_axis=1, tiled=True
    )
    local_sums = lax.dot_general(
        picker_half, back_rows, (((0,), (1,)), ((), ())), preferred_element_type=jnp.float32
    )
    grad_in = lax.psum_scatter(
        local_sums.astype(jnp.bfloat16), "tensor", scatter_dimension=1, tiled=True
    )
    position = jnp.where(occupied, entries, tok_count * top_count)
    gate_sums = (
        jnp.zeros((tok_count * top_count + 1,), jnp.float32).at[position].add(back_gate.reshape(-1))
    )
    grad_gate = gate_sums[:-1].reshape(tok_count, top_count)
    return (grad_in, grad_gate)


NZ, NY, NX, NC = 4, 2, 2, 2


def _pairs(move):
    pairs = []
    for z in range(NZ):
        for y in range(NY):
            for x in range(NX):
                for c in range(NC):
                    tz, ty, tx, tc = move(z, y, x, c)
                    pairs.append((((z * NY + y) * NX + x) * NC + c, ((tz * NY + ty) * NX + tx) * NC + tc))
    return pairs


TO_X = _pairs(lambda z, y, x, c: (z, y, 1 - x, c))
TO_Y = _pairs(lambda z, y, x, c: (z, 1 - y, x, c))
TO_CORE = _pairs(lambda z, y, x, c: (z, y, x, 1 - c))
LEFT = _pairs(lambda z, y, x, c: (z, y, 1 - x, c) if c == 0 else (z, 1 - y, x, c))
RIGHT = _pairs(lambda z, y, x, c: (z, 1 - y, x, c) if c == 0 else (z, y, 1 - x, c))
TO_Z = [_pairs(lambda z, y, x, c, d=d: (z ^ d, y, x, c)) for d in range(NZ)]
CHUNKS = ((0, 2), (1, 3))


def send(value, pairs, name="send"):
    with jax.named_scope(name):
        return lax.ppermute(value, BOTH, pairs)


def after(value, *first):
    return lax.optimization_barrier((value, *first))[0]


def dot_nt(a, b):
    return lax.dot_general(a, b, (((1,), (1,)), ((), ())), preferred_element_type=F32)


def shape_of(shape, dtype):
    return jax.ShapeDtypeStruct(shape, dtype)


HINT = pl.CostEstimate(flops=0, transcendentals=0, bytes_accessed=0)
SMALL = pltpu.CompilerParams(vmem_limit_bytes=40 << 20)
LARGE = pltpu.CompilerParams(vmem_limit_bytes=48 << 20)


def kernel(name, body, outs, grid, in_specs, out_specs, *args, scratch=()):
    return pl.pallas_call(
        body,
        out_shape=outs,
        grid_spec=pltpu.PrefetchScalarGridSpec(
            num_scalar_prefetch=1, grid=grid, in_specs=in_specs, out_specs=out_specs, scratch_shapes=scratch
        ),
        compiler_params=LARGE if name in ("hidden", "input") else SMALL,
        cost_estimate=HINT,
        name=name,
    )(*args)


META = 8


def pack_rows(grad_out, slots, gates):
    tokens, quarter = grad_out.shape
    experts = slots.shape[0]
    top_count = gates.shape[0]

    def body(g_ref, s_ref, w_ref, out, choice_ref):
        out[:tokens] = g_ref[...]
        entries = s_ref[...]
        owner = lax.div(entries, top_count)
        choice = (entries - owner * top_count).astype(F32)
        owner = owner.astype(F32)
        gate = w_ref[...].astype(F32)
        square = lax.broadcasted_iota(jnp.int32, (tokens, tokens), 0).astype(F32)
        row = lax.broadcasted_iota(jnp.int32, (META, tokens), 0)
        lane = lax.broadcasted_iota(jnp.int32, (META, tokens), 1).astype(F32)
        number = lax.broadcasted_iota(jnp.int32, (top_count, tokens), 0).astype(F32)
        for e in range(experts):
            hit = jnp.where(square == owner[e : e + 1], 1.0, 0.0).astype(BF16)
            value = jnp.where(row == 0, lane, choice[e : e + 1]).astype(BF16)
            found = dot_nt(value, hit)
            chosen = found[1:2]
            weight = jnp.sum(jnp.where(number == chosen, gate, 0.0), axis=0, keepdims=True)
            choice_ref[e : e + 1, :] = chosen
            out[tokens:, e * tokens : (e + 1) * tokens] = jnp.where(row == 0, found, weight).astype(BF16)

    full = lambda shape: pl.BlockSpec(shape, lambda i: (0, 0))
    return pl.pallas_call(
        body,
        out_shape=[shape_of((tokens + META, quarter), BF16), shape_of((experts, tokens), F32)],
        grid=(1,),
        in_specs=[full(grad_out.shape), full(slots.shape), full(gates.shape)],
        out_specs=[full((tokens + META, quarter)), full((experts, tokens))],
        compiler_params=pltpu.CompilerParams(vmem_limit_bytes=60 << 20),
        cost_estimate=HINT,
        name="pack",
    )(grad_out, slots, gates)


def prepare(expert, block, near, saved_gate, saved_up, chunk):
    tokens = near[0][0].shape[0] - META
    hid = saved_gate.shape[1]
    count = len(chunk)
    low, step = chunk[0], chunk[1] - chunk[0]

    def group(i, e, s):
        return ((e[0] // NY) ^ (low + step * (i % count))) * NY + ((e[0] % NY) ^ (i // count))

    def body(e_ref, s_ref, *refs):
        metas = refs[: 3 * count]
        g_ref, u_ref = refs[3 * count : 3 * count + 2]
        outs = refs[3 * count + 2 :]
        i, c = pl.program_id(0), s_ref[0] % NC
        meta = None
        for k in range(count):
            own, first, second = (m[...].astype(F32) for m in metas[3 * k : 3 * k + 3])
            mine = jnp.where(i // count == 0, own, jnp.where(c == 0, first, second))
            meta = mine if meta is None else jnp.where(i % count == k, mine, meta)
        slots = lax.broadcasted_iota(jnp.int32, (tokens, tokens), 0).astype(F32)
        pick = jnp.where(slots == meta[0:1], 1.0, 0.0).astype(BF16)
        flip = (((0,), (0,)), ((), ()))
        gate_pre = lax.dot_general(pick, g_ref[...], flip, preferred_element_type=F32)
        up_pre = lax.dot_general(pick, u_ref[...], flip, preferred_element_type=F32)
        scale = jnp.transpose(jnp.broadcast_to(meta[1:2], (tokens, tokens)))[:, 0:1]
        activated, derivative = silu_pair(gate_pre)
        outs[0][...] = activated * up_pre
        outs[1][...] = scale * up_pre * derivative
        outs[2][...] = scale * activated

    out = shape_of((NY * count * tokens, hid), F32)
    meta = pl.BlockSpec((META, tokens), lambda i, e, s: (tokens // META, e[0]))
    saved = pl.BlockSpec((tokens, hid), lambda i, e, s: (group(i, e, s), 0))
    spec = pl.BlockSpec((tokens, hid), lambda i, e, s: (i, 0))
    flat = [p for three in near for p in three]
    return pl.pallas_call(
        body,
        out_shape=[out] * 3,
        grid_spec=pltpu.PrefetchScalarGridSpec(
            num_scalar_prefetch=2,
            grid=(NY * count,),
            in_specs=[meta] * len(flat) + [saved, saved],
            out_specs=[spec] * 3,
        ),
        compiler_params=LARGE,
        cost_estimate=HINT,
        name="prepare",
    )(expert, block, *flat, saved_gate, saved_up)


def hidden_parts(block, pieces, down, got):
    tokens, quarter = pieces[0][0].shape[0] - META, pieces[0][0].shape[1]
    hid = down.shape[0]
    count = len(pieces)
    half = count * tokens
    rows = NY * half
    steps = 2
    wide = quarter // steps

    def body(s_ref, *refs):
        near = refs[: 4 * count]
        d_ref, o_ref, mine, theirs, rows_v, w_v, row_sem, w_sem = refs[4 * count :]
        x, c = s_ref[0] // NC, s_ref[0] % NC

        def weight(dx, h, k):
            first = pl.multiple_of((2 * (x ^ dx) + c) * quarter + h * wide, wide)
            source = (d_ref, o_ref)[k].at[:, pl.ds(first, wide)]
            return pltpu.make_async_copy(source, w_v.at[dx, h, pl.ds(k * hid, hid), :], w_sem.at[dx, h, k])

        def piece(i, j, dx, h, dy):
            target = rows_v.at[dx, h, pl.ds(dy * half + i * tokens, tokens), :]
            source = near[4 * i + j].at[pl.ds(0, tokens), pl.ds(h * wide, wide)]
            return pltpu.make_async_copy(source, target, row_sem.at[i, dx, h, dy])

        def begin(dx, h):
            for k in (1, 0):
                weight(dx, h, k).start()
            for i in range(count):
                piece(i, 0 if dx == 0 else 3, dx, h, dx).start()

                @pl.when(c == dx)
                def _(i=i, dx=dx, h=h):
                    piece(i, 1, dx, h, 1 - dx).start()

                @pl.when(c != dx)
                def _(i=i, dx=dx, h=h):
                    piece(i, 2, dx, h, 1 - dx).start()

        order = [(dx, h) for dx in range(NX) for h in range(steps)]
        begin(*order[0])
        begin(*order[1])
        total = None
        for n, (dx, h) in enumerate(order):
            for i in range(count):
                for dy in range(NY):
                    piece(i, 0, dx, h, dy).wait()
            for k in (1, 0):
                weight(dx, h, k).wait()
            if n + 2 < len(order):
                begin(*order[n + 2])
            part = dot_nt(rows_v[dx, h], w_v[dx, h])
            total = part if n == 0 else total + part
        mine[...] = total[:, :hid]
        theirs[...] = total[:, hid:].astype(BF16)

    flat = [p for four in pieces for p in four]
    spec = lambda cols: pl.BlockSpec((rows, cols), lambda i, s: (0, 0))
    return kernel(
        "hidden",
        body,
        [shape_of((rows, hid), F32), shape_of((rows, hid), BF16)],
        (1,),
        [pl.BlockSpec(memory_space=pl.ANY)] * (len(flat) + 2),
        [spec(hid)] * 2,
        block,
        *flat,
        down,
        got,
        scratch=[
            pltpu.VMEM((NX, steps, rows, wide), BF16),
            pltpu.VMEM((NX, steps, 2 * hid, wide), BF16),
            pltpu.SemaphoreType.DMA((count, NX, steps, NY)),
            pltpu.SemaphoreType.DMA((NX, steps, 2)),
        ],
    )


def pre_grads(block, mine, back, factors):
    rows, hid = mine.shape
    half = rows // NY
    count = len(CHUNKS[0])
    tokens = half // count

    def body(s_ref, m_ref, b_ref, f0, f1, f2, h_ref, t_ref):
        bh = m_ref[...] + b_ref[...].astype(F32)
        h_ref[:, :hid] = (bh * f1[...]).astype(BF16)
        h_ref[:, hid:] = (bh * f2[...]).astype(BF16)
        term = jnp.sum(bh * f0[...], axis=1, keepdims=True)
        flat = jnp.transpose(jnp.broadcast_to(term, (half, 128)))
        for i in range(count):
            t_ref[0, i : i + 1, :] = flat[0:1, i * tokens : (i + 1) * tokens]

    outs = [shape_of((rows, 2 * hid), BF16), shape_of((NY, count, tokens), F32)]
    spec = lambda cols: pl.BlockSpec((half, cols), lambda i, s: (i, 0))
    return kernel(
        "pre_grads",
        body,
        outs,
        (NY,),
        [spec(hid)] * 5,
        [spec(2 * hid), pl.BlockSpec((1, count, tokens), lambda i, s: (i, 0, 0))],
        block,
        mine,
        back,
        *factors,
    )


def input_parts(block, mine, theirs, weights, got):
    rows = mine.shape[0] // NY
    hid = mine.shape[1] // 2
    quarter = weights[0].shape[0] // (NX * NC)
    steps = 2
    wide = quarter // steps
    order = [(dx, h) for dx in (1, 0) for h in range(steps)]

    def body(s_ref, m_ref, t_ref, *refs):
        sources = refs[:4]
        outs = refs[4:8]
        side_v, w_v, o_v, side_sem, sem, out_sem = refs[8:]
        x, c = s_ref[0] // NC, s_ref[0] % NC

        def weight(n, j):
            dx, h = order[n]
            first = pl.multiple_of((2 * (x ^ dx) + c) * quarter + h * wide, wide)
            target = w_v.at[n, j // 2, :, pl.ds((j % 2) * hid, hid)]
            return pltpu.make_async_copy(sources[j].at[pl.ds(first, wide), :], target, sem.at[n, j])

        def side(k):
            return pltpu.make_async_copy((m_ref, t_ref)[k], side_v.at[k], side_sem.at[k])

        def give(which, n, dy):
            cols = pl.ds(order[n][1] * wide, wide)
            return pltpu.make_async_copy(o_v.at[n, dy], outs[which].at[:, cols], out_sem.at[n, dy])

        side(0).start()
        for j in range(4):
            weight(0, j).start()
        side(1).start()
        for j in range(4):
            weight(1, j).start()
        side(0).wait()
        for n, (dx, h) in enumerate(order):
            total = None
            for k in range(2):
                for j in (2 * k, 2 * k + 1):
                    weight(n, j).wait()
                if n == 0 and k == 1:
                    side(1).wait()
                part = dot_nt(side_v[k], w_v[n, k])
                total = part if k == 0 else total + part
                for j in (2 * k, 2 * k + 1):
                    if n + 2 < len(order):
                        weight(n + 2, j).start()
            o_v[n, 0] = total[:rows].astype(BF16)
            o_v[n, 1] = total[rows:].astype(BF16)
            give(0 if dx == 1 else 3, n, dx).start()

            @pl.when(c == 1 - dx)
            def _(n=n, dx=dx):
                give(1, n, 1 - dx).start()

            @pl.when(c != 1 - dx)
            def _(n=n, dx=dx):
                give(2, n, 1 - dx).start()

        for n in range(len(order)):
            for dy in range(NY):
                give(0, n, dy).wait()

    far = pl.BlockSpec(memory_space=pl.ANY)
    return kernel(
        "input",
        body,
        [shape_of((rows, quarter), BF16)] * 4,
        (1,),
        [far] * 6,
        [far] * 4,
        block,
        mine,
        theirs,
        *weights,
        *got,
        scratch=[
            pltpu.VMEM((2,) + mine.shape, BF16),
            pltpu.VMEM((len(order), 2, wide, 2 * hid), BF16),
            pltpu.VMEM((len(order), NY, rows, wide), BF16),
            pltpu.SemaphoreType.DMA((2,)),
            pltpu.SemaphoreType.DMA((len(order), 4)),
            pltpu.SemaphoreType.DMA((len(order), NY)),
        ],
    )


def add_pieces(block, base, first, second, types):
    rows, cols = base.shape
    part = rows // len(types)
    wide = cols

    def body(s_ref, b_ref, f_ref, g_ref, *outs):
        for i, out in enumerate(outs):
            s = slice(i * part, (i + 1) * part)
            out[...] = (b_ref[s].astype(F32) + f_ref[s].astype(F32) + g_ref[s].astype(F32)).astype(out.dtype)

    spec = lambda n: pl.BlockSpec((n, wide), lambda i, s: (0, i))
    outs = [shape_of((part, cols), t) for t in types]
    return kernel("add", body, outs, (1,), [spec(rows)] * 3, [spec(part)] * len(outs), block, base, first, second)


def add_corner(block, base, corner):
    rows, cols = base.shape

    def body(s_ref, b_ref, c_ref, out):
        out[...] = (b_ref[...].astype(F32) + c_ref[...].astype(F32)).astype(BF16)

    spec = pl.BlockSpec((rows, cols), lambda i, s: (0, i))
    return kernel("corner", body, shape_of(base.shape, BF16), (1,), [spec] * 2, spec, block, base, corner)


def last_sum(block, keep, parts, out_type):
    def body(s_ref, k_ref, *refs):
        total = k_ref[...]
        for ref in refs[:-1]:
            total = total + ref[...].astype(F32)
        refs[-1][...] = total.astype(out_type)

    spec = pl.BlockSpec(keep.shape, lambda i, s: (0, 0))
    return kernel(
        "last", body, shape_of(keep.shape, out_type), (1,), [spec] * (1 + len(parts)), spec, block, keep, *parts
    )


def dense_local(grad_out, gate_weights, slot_lists, saved_gate, saved_up, w_gate, w_up, w_down):
    tokens, quarter = grad_out.shape
    experts = slot_lists.shape[1]
    top_count = gate_weights.shape[1]
    expert = lax.axis_index("expert")
    block = lax.axis_index("tensor")
    z, y = expert // NY, expert % NY
    at_expert, at_block = expert.reshape(1), block.reshape(1)

    down, gate_w, up_w = w_down[0], w_gate[0], w_up[0]
    near, far = CHUNKS
    own, choice_of = pack_rows(grad_out, slot_lists[0], gate_weights.T)

    z2, z1 = send(own, TO_Z[2], "z2"), send(own, TO_Z[1], "z1")
    first0, second0 = send(own, RIGHT, "first0"), send(own, LEFT, "second0")
    got_down = send(down, TO_CORE, "weights")

    z2, z1, first0, second0, got_down, gate_w_, up_w_ = lax.optimization_barrier(
        (z2, z1, first0, second0, got_down, gate_w, up_w)
    )
    first2, second2 = send(z2, RIGHT, "first2"), send(z2, LEFT, "second2")
    third0 = send(first0, LEFT, "third0")
    z3 = send(z2, TO_Z[1], "z3")
    got_gate = send(gate_w_, TO_CORE, "weights")

    z1, z3, first2, second2, third0, got_gate, up_w_ = lax.optimization_barrier(
        (z1, z3, first2, second2, third0, got_gate, up_w_)
    )
    got_up = send(up_w_, TO_CORE, "weights")
    third2 = send(first2, LEFT, "third2")
    first1, second1 = send(z1, RIGHT, "first1"), send(z1, LEFT, "second1")
    first3 = send(z3, RIGHT, "first3")
    saved = saved_gate[0], saved_up[0]
    factors_a = prepare(
        at_expert, at_block, [(own, first0, second0), (z2, first2, second2)], *saved, near
    )
    place = after(at_block, factors_a[0])

    weights, got = (gate_w, up_w), (got_gate, got_up)

    def stage_corner(place, chunk, left, corner):
        value = add_corner(place, left, corner)
        return send(value, RIGHT, f"r_left{chunk[0]}"), value

    def stage_add(place, chunk, base, right, left):
        types = [F32 if d == 0 else BF16 for d in chunk]
        totals = add_pieces(place, base, right, left, types)
        return {d: t if d == 0 else send(t, TO_Z[d], f"r_z{d}") for d, t in zip(chunk, totals)}, totals[0]

    mine, theirs = hidden_parts(
        place, [(own, first0, second0, third0), (z2, first2, second2, third2)], down, got_down
    )
    theirs, first1, second1, got_up, first3 = lax.optimization_barrier((theirs, first1, second1, got_up, first3))
    back = send(theirs, TO_CORE, "swap_bh0")
    second3 = send(z3, LEFT, "second3")
    third3 = send(first3, LEFT, "third3")
    third1 = send(first1, LEFT, "third1")
    mine, term_a = pre_grads(after(at_block, mine), mine, back, factors_a)
    theirs = send(mine, TO_CORE, "swap_h0")
    place = at_block
    corner_a, right_a, left_a, base_a = input_parts(place, mine, theirs, weights, got)
    place = after(at_block, base_a)
    corner_a, right_a = send(corner_a, LEFT, "r_corner0"), send(right_a, LEFT, "r_right0")

    factors_b = prepare(
        at_expert, place, [(z1, first1, second1), (z3, first3, second3)], *saved, far
    )
    place = after(at_block, factors_b[0])
    mine, theirs = hidden_parts(
        place, [(z1, first1, second1, third1), (z3, first3, second3, third3)], down, got_down
    )
    back = send(theirs, TO_CORE, "swap_bh1")
    place = after(at_block, mine)
    left_a, value = stage_corner(place, near, left_a, corner_a)
    place = after(at_block, value)
    mine, term_b = pre_grads(place, mine, back, factors_b)
    theirs = send(mine, TO_CORE, "swap_h1")
    place = at_block
    corner_b, right_b, left_b, base_b = input_parts(place, mine, theirs, weights, got)
    place = after(at_block, base_b)
    corner_b, right_b = send(corner_b, LEFT, "r_corner1"), send(right_b, LEFT, "r_right1")
    sums, value = stage_add(place, near, base_a, right_a, left_a)
    left_b, value = stage_corner(after(at_block, value), far, left_b, corner_b)
    early = sums[2]
    more, kept = stage_add(after(at_block, value), far, base_b, right_b, left_b)
    sums.update(more)
    grad_in = last_sum(at_block, sums[0], [sums[d] for d in (2, 1, 3)], BF16)

    terms = {d: t[:, i] for c, t in ((near, term_a), (far, term_b)) for i, d in enumerate(c)}
    term = jnp.stack([terms[d] for d in range(NZ)], axis=1)
    term = term + send(term, TO_CORE, "t_core")
    term = term + send(after(term, base_b), TO_X, "t_x")
    term = after(term, value)
    term = jnp.stack([term[0], send(term[1], TO_Y, "t_y")], axis=1)
    term = after(term, kept, early)
    slots = [term[0]] + [send(term[d], TO_Z[d], f"t_z{d}") for d in range(1, NZ)]
    slot_grad = jnp.zeros((experts, tokens), F32)
    ids = jnp.arange(experts, dtype=jnp.int32)
    for d in range(NZ):
        for dy in range(NY):
            source = (z ^ d) * NY + (y ^ dy)
            slot_grad = jnp.where((ids == source)[:, None], slots[d][dy][None], slot_grad)
    choice_ids = jnp.arange(top_count, dtype=F32)
    chosen = choice_of[:, :, None] == choice_ids[None, None, :]
    grad_gate = jnp.sum(jnp.where(chosen, slot_grad[:, :, None], 0.0), axis=0)
    return (grad_in, grad_gate)


def local(grad_out, gate_weights, slot_lists, *rest):
    tokens = grad_out.shape[0]
    _, experts, capacity = slot_lists.shape
    dense = experts == gate_weights.shape[1] == NZ * NY and capacity == tokens
    dense = dense and lax.axis_size("expert") == NZ * NY and lax.axis_size("tensor") == NX * NC
    program = dense_local if dense else routed_local
    return program(grad_out, gate_weights, slot_lists, *rest)


def solution(mesh):
    in_specs = (
        P("expert", "tensor"),
        P("expert", None),
        P("expert", None, None),
        P("expert", None, "tensor"),
        P("expert", None, "tensor"),
        P("expert", None, "tensor"),
        P("expert", None, "tensor"),
        P("expert", "tensor", None),
    )
    out_specs = (P("expert", "tensor"), P("expert", None))
    return jax.shard_map(local, mesh=mesh, in_specs=in_specs, out_specs=out_specs, check_vma=False)
```
